32 devices in a mesh: layer: 4 (over y, x), row: 2 (over core), col: 4 (over z).
Axes of the slice: x: 2, y: 2, z: 4, core: 2. Of those that a mesh axis runs over, the one named last changes fastest.
Arguments:
- cols: int32 [64, 16], P(('row', 'col'), 'layer'), may hold values from -1 to 63, as said below
- vals: bfloat16 [64, 16, 256, 256], P(('row', 'col'), 'layer'), as said below
- outcols: int32 [64, 4], P(('row', 'col')), may hold values from -1 to 63, as said below
Outputs:
- purified: bfloat16 [64, 4, 256, 256], P(('row', 'col'), 'layer')
The draws below stay inside these ranges and needn't reach their ends.
Inputs may be any that keep to these rules, and one draw needn't show every extreme that they name: `cols`: slots 4 * l to 4 * l + 3 of block row i hold distinct block columns k with k mod 4 = l and |k - i| <= 6, or -1. Column i is always listed in row i, and k is listed in row i exactly when i is listed in row k. vals[i, s] is block (i, cols[i, s]) of a symmetric matrix: the block listed at (k, i) is the transpose of the one at (i, k). Slots holding -1 hold zeros. `outcols`: block row i lists distinct block columns j with i <= j <= i + 12, always i itself, or -1.
All inputs are finite; a program needn't handle non-finite values.
Results may differ from the reference program's by a relative error of at most 0.0085.
Values may be sent and summed in bfloat16 or wider, within the bound.
A program may use at most 64 MiB of HBM per device.

```python
import jax
import jax.numpy as jnp
from jax import lax

B = 256
W = 6
KL = 4
KO = 4
GROUPS = 4
NB = 64


def make_cols(key):
    base_key = jax.random.fold_in(key, 11)
    first_key, second_key = jax.random.split(base_key)
    regions = (NB + 7) // 8
    region = jnp.arange(NB) // 8
    limits = jax.random.randint(first_key, (regions,), 35, 100)[region]
    rolls = jax.random.randint(second_key, (NB, W), 0, 100)
    index = jnp.arange(NB)[:, None]
    offsets = jnp.arange(1, W + 1)[None, :]
    upper = (rolls < limits[:, None]) & (index + offsets < NB)
    source = jnp.clip(index - offsets, 0, NB - 1)
    lower = upper[source, offsets - 1] & (index - offsets >= 0)
    table = jnp.concatenate([lower[:, ::-1], jnp.ones((NB, 1), dtype=bool), upper], axis=1)
    group = jnp.arange(GROUPS)[None, :, None]
    step = jnp.arange(KL)[None, None, :]
    rowid = jnp.arange(NB)[:, None, None]
    start = rowid - W + jnp.mod(group - (rowid - W), GROUPS)
    column = start + step * GROUPS
    offset = column - rowid
    inside = (offset <= W) & (column >= 0) & (column < NB)
    listed = jnp.take_along_axis(table, jnp.clip(offset + W, 0, 2 * W).reshape(NB, -1), axis=1).reshape(NB, GROUPS, KL)
    chosen = jnp.where(inside & listed, column, -1)
    return chosen.reshape(NB, GROUPS * KL).astype(jnp.int32)


def block_value(key, first, distance):
    block_key = jax.random.fold_in(jax.random.fold_in(jax.random.fold_in(key, 41), first), distance)
    raw = jax.random.normal(block_key, (B, B), jnp.float32)
    raw = 0.1 * raw
    return jnp.where(distance == 0, 0.70710678 * (raw + raw.T), raw)


def draw_cols(key, part):
    return make_cols(key)


def draw_vals(key, part):
    listing = make_cols(key)

    def one_row(index):
        columns = listing[index]
        first = jnp.minimum(index, columns)
        distance = jnp.abs(columns - index)
        blocks = jax.vmap(lambda a, d: block_value(key, a, d))(jnp.clip(first, 0, NB - 1), distance)
        flipped = jnp.swapaxes(blocks, 1, 2)
        blocks = jnp.where((columns < index)[:, None, None], flipped, blocks)
        blocks = jnp.where((columns >= 0)[:, None, None], blocks, jnp.float32(0.0))
        return blocks.astype(jnp.bfloat16)
    return lax.map(one_row, jnp.arange(NB, dtype=jnp.int32))


def draw_outcols(key, part):
    score_key = jax.random.fold_in(key, 53)
    width = 2 * W + 1
    scores = jax.random.randint(score_key, (NB, width), 0, 1000) * 32 + jnp.arange(width)[None, :]
    scores = scores + jnp.where(jnp.arange(width)[None, :] == 0, 1000000, 0)
    rowid = jnp.arange(NB)[:, None]
    scores = jnp.where(rowid + jnp.arange(width)[None, :] < NB, scores, -1)
    best, picked = lax.top_k(scores, KO)
    return jnp.where(best >= 0, rowid + picked, -1).astype(jnp.int32)


def setup_inputs(seed: int = 0) -> dict:
    arg_keys = jax.random.split(jax.random.key(seed), 4)
    return {
        "cols": draw_cols(jax.random.fold_in(arg_keys[3], 71), 0),
        "vals": draw_vals(jax.random.fold_in(arg_keys[3], 71), 0),
        "outcols": draw_outcols(jax.random.fold_in(arg_keys[3], 71), 0),
    }


def reference(cols, vals, outcols):
    nrows = vals.shape[0]
    groups = cols.shape[1] // KL

    def one_row(index):
        left = vals[index].astype(jnp.float32).reshape(groups, KL, B, B)
        left_cols = cols[index].reshape(groups, KL)
        targets = outcols[index]
        where = jnp.clip(targets, 0, nrows - 1).astype(jnp.int32)
        right = vals[where].astype(jnp.float32).reshape(KO, groups, KL, B, B)
        right_cols = cols[where].reshape(KO, groups, KL)
        hits = ((left_cols[None, :, :, None] == right_cols[:, :, None, :]) & (left_cols[None, :, :, None] >= 0)).astype(jnp.float32)
        moved = jnp.einsum('ogst,ogtab->ogsab', hits, right)
        product = jnp.einsum('gsab,ogscb->ogac', left, moved)
        owned = (left_cols[None, :, :] == targets[:, None, None]).astype(jnp.float32)
        twice = 2.0 * jnp.einsum('ogs,gsab->ogab', owned, left)
        rounded = lax.optimization_barrier((twice - product).astype(jnp.bfloat16))
        total = jnp.sum(rounded.astype(jnp.float32), axis=1)
        total = jnp.where(targets[:, None, None] >= 0, total, jnp.float32(0.0))
        return total.astype(jnp.bfloat16)

    return lax.map(one_row, jnp.arange(nrows, dtype=jnp.int32))
```

```python
import functools

import jax
import jax.numpy as jnp
from jax import lax
from jax.experimental import pallas as pl
from jax.experimental.pallas import tpu as pltpu
from jax.sharding import PartitionSpec as P

W = 6
MESH = pl.DeviceIdType.MESH

LOCAL = (
    ((3, 0), (2, 0), (5, 0), (6, 0), (6, 4), (7, 0), (7, 4)),
    ((3, 1), (4, 1), (6, 1), (7, 1), (7, 5)),
    ((4, 2), (5, 2), (7, 2)),
    ((5, 3), (6, 3)),
)
LOCAL_BELOW = ()
FORWARD = ((1, 0), (2, 0), (3, 1), (3, 2))
X_FIRST = (True, False, True, False, True, False, True, False)


def kernel(
    sizes, cols_hbm, targets_hbm, vals_hbm, out_ref,
    cols_ref, targets_ref, targets_up, right, pack, halo, lent, terms_out, terms_in,
    part, own, kept, recv,
    load_sem, pack_send, halo_recv, forward_send, lent_send, lent_recv, target_send, target_recv,
    term_send, term_recv, part_send, part_recv,
):
    rows, slots, outs, layers, groups, fine = sizes
    far = 2 * W
    layer = lax.axis_index("layer")
    group = lax.axis_index("row") * fine + lax.axis_index("col")
    base = group * rows
    zero_at = rows * slots
    halo_at = zero_at + 1
    has_above = group < groups - 1
    has_below = group > 0

    def group_id(by):
        other = (group + by + groups) % groups
        return {"row": other // fine, "col": other % fine}

    below, above = group_id(-1), group_id(1)

    def sel(values):
        if len(set(values)) == 1:
            return jnp.int32(values[0])
        out = jnp.int32(values[-1])
        for n in range(len(values) - 1):
            out = jnp.where(layer == n, values[n], out)
        return out

    def among(which):
        which = sorted(set(which))
        if len(which) == layers:
            return None
        cond = layer == which[0]
        for n in which[1:]:
            cond = cond | (layer == n)
        return cond

    def guard(which, *more):
        conds = [c for c in (among(which), *more) if c is not None]
        def wrap(f):
            if not conds:
                f()
                return
            cond = conds[0]
            for c in conds[1:]:
                cond = cond & c
            pl.when(cond)(f)
        return wrap

    def find(row, column):
        slot = jnp.int32(0)
        hit = jnp.int32(0)
        for s in range(slots):
            same = (cols_ref[s, row] == column).astype(jnp.int32)
            slot = slot + s * same
            hit = hit + same
        return jnp.minimum(slot, slots - 1), hit

    def block_of(row, column):
        slot, hit = find(row, base + column)
        block = right[row * slots + slot]
        return jnp.where(hit > 0, block, jnp.zeros_like(block))

    lists = [[] for _ in range(layers)]
    for k, t in LOCAL_BELOW:
        lists[k % layers].append((k, t))
    forwarded = {(rows + b, a) for a, b in FORWARD}
    for n in range(layers):
        k = rows + n
        mine = [(k, t) for t in range(min(k - rows + W + 1, rows)) if (k, t) not in forwarded]
        early = [(rows + a, b) for a, b in FORWARD if a == n]
        lists[n] += early + [e for e in mine if e not in early]
    crossing = [[e for e in LOCAL[n] if e not in LOCAL_BELOW] for n in range(layers)]
    down_most = max(len(x) for x in lists)
    cross_most = max(len(x) for x in crossing)
    lent_at = down_most + cross_most

    def at_of(k, t):
        return k // layers * far + t

    def down_copy(n):
        at = sel([at_of(*x[n]) if n < len(x) else 0 for x in lists])
        return pltpu.make_async_remote_copy(
            src_ref=pack.at[n], dst_ref=halo.at[at], send_sem=pack_send.at[n], recv_sem=halo_recv.at[at],
            device_id=below, device_id_type=MESH,
        )

    def down_has(n):
        return [m for m in range(layers) if n < len(lists[m])]

    def cross_copy(n):
        at = sel([at_of(*x[n]) if n < len(x) else 0 for x in crossing])
        to = sel([x[n][0] % layers if n < len(x) else 0 for x in crossing])
        return pltpu.make_async_remote_copy(
            src_ref=pack.at[down_most + n], dst_ref=halo.at[at],
            send_sem=pack_send.at[down_most + n], recv_sem=halo_recv.at[at],
            device_id={"layer": to}, device_id_type=MESH,
        )

    def cross_has(n):
        return [m for m in range(layers) if n < len(crossing[m])]

    def lent_copy(i):
        return pltpu.make_async_remote_copy(
            src_ref=pack.at[lent_at + i], dst_ref=lent.at[i], send_sem=lent_send.at[i], recv_sem=lent_recv.at[i],
            device_id=above, device_id_type=MESH,
        )

    def target_copy():
        return pltpu.make_async_remote_copy(
            src_ref=targets_ref, dst_ref=targets_up, send_sem=target_send, recv_sem=target_recv,
            device_id=above, device_id_type=MESH,
        )

    def forward_copy(n):
        a, b = FORWARD[n]
        return pltpu.make_async_remote_copy(
            src_ref=halo.at[at_of(rows + a, b)], dst_ref=halo.at[at_of(rows + b, a)],
            send_sem=forward_send.at[n], recv_sem=halo_recv.at[at_of(rows + b, a)],
            device_id={"layer": jnp.int32(b)}, device_id_type=MESH,
        )

    passed = [(k, t) for k in range(layers) for t in range(k - rows + W + 1)]

    def pass_copy(n):
        k, t = passed[n]
        return pltpu.make_async_remote_copy(
            src_ref=halo.at[at_of(k, t)], dst_ref=halo.at[at_of(rows + k, rows + t)],
            send_sem=forward_send.at[len(FORWARD) + n], recv_sem=halo_recv.at[at_of(rows + k, rows + t)],
            device_id=below, device_id_type=MESH,
        )

    def term_copy(n):
        return pltpu.make_async_remote_copy(
            src_ref=terms_out.at[n], dst_ref=terms_in.at[n], send_sem=term_send.at[n], recv_sem=term_recv.at[n],
            device_id=below, device_id_type=MESH,
        )

    def part_copy(at, to):
        return pltpu.make_async_remote_copy(
            src_ref=part.at[at], dst_ref=recv.at[at], send_sem=part_send.at[at], recv_sem=part_recv.at[at],
            device_id={"layer": to}, device_id_type=MESH,
        )

    lx, ly = layer % 2, layer // 2
    flip_x, flip_y, both = ly * 2 + 1 - lx, (1 - ly) * 2 + lx, (1 - ly) * 2 + 1 - lx

    def mates(row):
        return (flip_x, flip_y) if X_FIRST[row] else (flip_y, flip_x)

    loads = [
        pltpu.make_async_copy(cols_hbm, cols_ref, load_sem.at[0]),
        pltpu.make_async_copy(targets_hbm, targets_ref, load_sem.at[1]),
        pltpu.make_async_copy(vals_hbm, right.at[pl.ds(0, rows * slots)], load_sem.at[2]),
    ]
    for load in loads:
        load.start()
    barrier = pltpu.get_barrier_semaphore()
    for r in range(1, layers):
        to = {"layer": (layer + r) % layers}
        pl.semaphore_signal(barrier, inc=1, device_id=to, device_id_type=MESH)

    @pl.when(has_below)
    def _():
        pl.semaphore_signal(barrier, inc=1, device_id=below, device_id_type=MESH)

    @pl.when(has_above)
    def _():
        pl.semaphore_signal(barrier, inc=1, device_id=above, device_id_type=MESH)

    right[zero_at] = jnp.zeros(right.shape[1:], right.dtype)
    for load in loads:
        load.wait()

    def cross_pack(n):
        @guard(cross_has(n), has_above)
        def _():
            row = sel([x[n][0] if n < len(x) else 0 for x in crossing])
            t = sel([x[n][1] if n < len(x) else 0 for x in crossing])
            pack[down_most + n] = block_of(row, rows + t).T

    def cross_start(n):
        @guard(cross_has(n), has_above)
        def _():
            cross_copy(n).start()

    def down_pack(n):
        @guard(down_has(n), has_below)
        def _():
            k = sel([x[n][0] if n < len(x) else 0 for x in lists])
            t = sel([x[n][1] if n < len(x) else 0 for x in lists])
            pack[n] = block_of(t, k - rows)

    def down_start(n):
        @guard(down_has(n), has_below)
        def _():
            down_copy(n).start()

    cross_pack(0)
    down_pack(0)
    pl.semaphore_wait(barrier, layers - 1 + has_below.astype(jnp.int32) + has_above.astype(jnp.int32))
    cross_start(0)
    down_start(0)

    @pl.when(has_above & (layer < 2))
    def _():
        target_copy().start()
        for i in range(2):
            @guard((0,) if i == 0 else (0, 1))
            def _(i=i):
                pack[lent_at + i] = block_of(W + i, rows + layers + layer)
                lent_copy(i).start()

    for n in range(1, max(down_most, cross_most)):
        if n < cross_most:
            cross_pack(n)
            cross_start(n)
        if n < down_most:
            down_pack(n)
            down_start(n)

    right[halo_at + far + layer] = block_of(layers + layer, rows + layer).T

    def arrive(k, t):
        @guard((k % layers,), group < groups - 2 if t >= rows else has_above)
        def _():
            at = at_of(k, t)
            pltpu.make_async_remote_copy(
                src_ref=halo.at[at], dst_ref=halo.at[at], send_sem=pack_send.at[0], recv_sem=halo_recv.at[at],
                device_id=below, device_id_type=MESH,
            ).wait_recv()
            block = halo[at]
            right[halo_at + at] = block.T if (k, t) in forwarded else block
            for n, (a, b) in enumerate(FORWARD):
                if (rows + a, b) == (k, t):
                    forward_copy(n).start()
            if (k, t) in passed:
                @pl.when(has_below)
                def _():
                    pass_copy(passed.index((k, t))).start()

    def product(row, o):
        target = targets_ref[o, row]
        there = target - base
        near = jnp.clip(there, 0, rows - 1)
        t = there - rows
        total = None
        for s in range(slots):
            column = cols_ref[s, row]
            slot, hit = find(near, column)
            local_at = jnp.where(hit > 0, near * slots + slot, zero_at)
            place = column - base
            q = (place - layer) // layers
            reach = (place >= t + rows - W) & (place < rows + layers) & (t < far)
            far_at = jnp.where(reach, halo_at + q * far + t, zero_at)
            at = jnp.where(there < rows, local_at, far_at)
            at = jnp.where((target >= 0) & (column >= 0), at, zero_at)
            at = jnp.clip(at, 0, right.shape[0] - 1)
            term = lax.dot_general(
                right[row * slots + s], right[at], (((1,), (1,)), ((), ())),
                preferred_element_type=jnp.float32,
            )
            total = term if total is None else total + term
        if row >= W:
            lends = ((layer == 0) | ((layer == 1) & (row > W))) & has_above
            theirs = terms_in[(row - W) * outs + o].astype(jnp.float32)
            total = total + jnp.where(lends, theirs, jnp.zeros_like(theirs))
        slot, hit = find(row, target)
        mine = (hit > 0) & (target >= 0)
        block = right[row * slots + jnp.where(mine, slot, 0)].astype(jnp.float32)
        twice = jnp.where(mine, 2.0 * block, jnp.zeros_like(block))
        return twice - total

    def terms(i):
        def body(o, carry):
            target = targets_up[o, W + i]
            there = target - base
            near = jnp.clip(there, 0, rows - 1)
            slot, hit = find(near, base + layers + layer)
            local_at = jnp.where(hit > 0, near * slots + slot, zero_at)
            t = there - rows
            reach = layers + layer >= t + rows - W
            far_at = jnp.where(reach, halo_at + far + t, zero_at)
            at = jnp.where(there < rows, local_at, far_at)
            at = jnp.where((target >= 0) & (there >= 0), at, zero_at)
            at = jnp.clip(at, 0, right.shape[0] - 1)
            term = lax.dot_general(
                lent[i], right[at], (((1,), (1,)), ((), ())), preferred_element_type=jnp.float32,
            )
            terms_out[i * outs + o] = term.astype(terms_out.dtype)
            term_copy(i * outs + o).start()
            return carry
        lax.fori_loop(0, outs, body, 0)

    def one_row(row):
        first, second = mates(row)
        part[2 * row + 1] = product(row, both).astype(part.dtype)
        part_copy(2 * row + 1, first).start()
        part[2 * row] = product(row, first).astype(part.dtype)
        part_copy(2 * row, first).start()
        kept[row] = product(row, second)
        own[row] = product(row, layer)

    def relay(row):
        first, second = mates(row)
        part_copy(2 * row + 1, first).wait_recv()
        total = kept[row] + recv[2 * row + 1].astype(jnp.float32)
        part[2 * rows + row] = total.astype(part.dtype)
        part_copy(2 * rows + row, second).start()

    needs = [[] for _ in range(rows + 2)]
    for q in range(2):
        for n in range(layers):
            k = q * layers + n
            for t in range(max(0, k - rows + W + 1)):
                if (t % layers) != n:
                    needs[0 if k < rows - 1 and t < far - rows + 1 else 1].append((k, t))
    fore = [(rows + a, b) for a, b in FORWARD]
    needs[1] += fore
    for n in range(layers):
        k = rows + n
        rest = [e for e in lists[n] if e[0] == k and e not in fore]
        rest += [e for e in sorted(forwarded) if e[0] == k]
        rest += [(k, t) for t in range(rows, k - rows + W + 1)]
        needs[2 + n] += rest

    relay_at = [[min(row + 2, rows) if row != 1 + n else 2 + n for row in range(rows)] for n in range(layers)]

    for row in range(rows):
        for at_row in range(rows):
            which = [n for n in range(layers) if relay_at[n][at_row] == row]
            if which:
                guard(which)(functools.partial(relay, at_row))
        if row == 2:
            @pl.when(has_below & (layer < 2))
            def _():
                target_copy().wait_recv()
                for i in range(2):
                    @guard((0,) if i == 0 else (0, 1))
                    def _(i=i):
                        lent_copy(i).wait_recv()
                        terms(i)
        for k, t in needs[row]:
            arrive(k, t)
        if row >= W:
            @guard((0,) if row == W else (0, 1), has_above)
            def _(row=row):
                for o in range(outs):
                    term_copy((row - W) * outs + o).wait_recv()
        one_row(row)
    for at_row in range(rows):
        which = [n for n in range(layers) if relay_at[n][at_row] >= rows]
        if which:
            guard(which)(functools.partial(relay, at_row))

    for row in range(rows):
        first, second = mates(row)
        part_copy(2 * row, first).wait_recv()
        part_copy(2 * rows + row, second).wait_recv()
        total = own[row] + recv[2 * row].astype(jnp.float32)
        total = total + recv[2 * rows + row].astype(jnp.float32)
        out_ref[row, 0] = total.astype(out_ref.dtype)

    for n in range(cross_most):
        guard(cross_has(n), has_above)(lambda n=n: cross_copy(n).wait_send())
    for n in range(down_most):
        guard(down_has(n), has_below)(lambda n=n: down_copy(n).wait_send())
    for n, (a, b) in enumerate(FORWARD):
        guard((a,), has_above)(lambda n=n: forward_copy(n).wait_send())
    for n, (k, t) in enumerate(passed):
        guard((k,), has_below, has_above)(lambda n=n: pass_copy(n).wait_send())

    @pl.when(has_above & (layer < 2))
    def _():
        target_copy().wait_send()
        for i in range(2):
            guard((0,) if i == 0 else (0, 1))(lambda i=i: lent_copy(i).wait_send())

    @pl.when(has_below & (layer < 2))
    def _():
        for i in range(2):
            @guard((0,) if i == 0 else (0, 1))
            def _(i=i):
                for o in range(outs):
                    term_copy(i * outs + o).wait_send()

    for row in range(rows):
        first, second = mates(row)
        part_copy(2 * row, first).wait_send()
        part_copy(2 * row + 1, first).wait_send()
        part_copy(2 * rows + row, second).wait_send()


def solution(mesh):
    layers = mesh.shape["layer"]
    fine = mesh.shape["col"]
    groups = mesh.shape["row"] * fine

    def per_device(cols, vals, outcols):
        rows, slots, size, _ = vals.shape
        outs = outcols.shape[1]
        assert rows == 2 * layers and rows == W + 2 and layers == 4 and outs == layers
        far = 2 * W
        block = (size, size)
        halo = 3 * far
        sent = 3 * rows
        packs = 20
        return pl.pallas_call(
            functools.partial(kernel, (rows, slots, outs, layers, groups, fine)),
            out_shape=jax.ShapeDtypeStruct((rows, outs // layers) + block, jnp.bfloat16),
            in_specs=[
                pl.BlockSpec(memory_space=pl.ANY),
                pl.BlockSpec(memory_space=pl.ANY),
                pl.BlockSpec(memory_space=pl.ANY),
            ],
            out_specs=pl.BlockSpec(memory_space=pltpu.VMEM),
            scratch_shapes=[
                pltpu.SMEM(cols.shape[::-1], cols.dtype),
                pltpu.SMEM(outcols.shape[::-1], outcols.dtype),
                pltpu.SMEM(outcols.shape[::-1], outcols.dtype),
                pltpu.VMEM((rows * slots + 1 + halo,) + block, jnp.bfloat16),
                pltpu.VMEM((packs,) + block, jnp.bfloat16),
                pltpu.VMEM((halo,) + block, jnp.bfloat16),
                pltpu.VMEM((2,) + block, jnp.bfloat16),
                pltpu.VMEM((2 * outs,) + block, jnp.bfloat16),
                pltpu.VMEM((2 * outs,) + block, jnp.bfloat16),
                pltpu.VMEM((sent,) + block, jnp.bfloat16),
                pltpu.VMEM((rows,) + block, jnp.float32),
                pltpu.VMEM((rows,) + block, jnp.float32),
                pltpu.VMEM((sent,) + block, jnp.bfloat16),
                pltpu.SemaphoreType.DMA((3,)),
                pltpu.SemaphoreType.DMA((packs,)),
                pltpu.SemaphoreType.DMA((halo,)),
                pltpu.SemaphoreType.DMA((12,)),
                pltpu.SemaphoreType.DMA((2,)),
                pltpu.SemaphoreType.DMA((2,)),
                pltpu.SemaphoreType.DMA,
                pltpu.SemaphoreType.DMA,
                pltpu.SemaphoreType.DMA((2 * outs,)),
                pltpu.SemaphoreType.DMA((2 * outs,)),
                pltpu.SemaphoreType.DMA((sent,)),
                pltpu.SemaphoreType.DMA((sent,)),
            ],
            compiler_params=pltpu.CompilerParams(collective_id=0, has_side_effects=True),
        )(cols.T, outcols.T, vals.reshape((rows * slots,) + block))

    in_specs = (
        P(("row", "col"), "layer"),
        P(("row", "col"), "layer", None, None),
        P(("row", "col"), None),
    )
    return jax.shard_map(
        per_device, mesh=mesh, in_specs=in_specs,
        out_specs=P(("row", "col"), "layer", None, None), check_vma=False,
    )
```

```python
import functools

import jax
import jax.numpy as jnp
from jax import lax
from jax.experimental import pallas as pl
from jax.experimental.pallas import tpu as pltpu
from jax.sharding import PartitionSpec as P

W = 6
MESH = pl.DeviceIdType.MESH

FAR_LEND, FAR_TERMS = 2, 4
LOCAL = (
    ((2, 0), (6, 0), (7, 0), (5, 0)),
    ((7, 5), (4, 1), (6, 1), (3, 1), (7, 1)),
    ((5, 2), (7, 2), (4, 2)),
    ((5, 3), (6, 3)),
)
BELOW = (
    ((8, 5), (8, 1), (8, 0), (8, 4), (8, 6)),
    ((9, 2), (9, 6), (9, 1), (9, 7), (9, 5), (9, 4), (9, 3)),
    ((10, 3), (6, 4), (10, 0), (10, 6), (10, 5), (10, 4), (10, 2), (10, 7)),
    ((11, 0), (3, 0), (11, 5), (7, 4), (11, 6), (11, 7), (11, 4), (11, 3)),
)
FORWARD = ((2, 0), (1, 3), (1, 2), (3, 0), (0, 1), (2, 3))
OVER_Y = (
    (0, 0, 1, 0),
    (0, 1, 0, 0),
    (1, 0, 1, 0),
    (0, 0, 0, 1),
    (1, 0, 1, 1),
    (0, 1, 0, 0),
    (1, 0, 1, 1),
    (1, 1, 0, 0),
)
STEPS = (
    (
        (('A', 8, 5), ('A', 4, 1), ('A', 4, 2)),
        (),
        (('A', 8, 1), ('T', 0, 0), ('A', 8, 0), ('A', 8, 3), ('A', 8, 4), ('R', 0, 0), ('A', 8, 2), ('A', 8, 6)),
        (),
        (),
        (('R', 0, 1),),
        (('R', 2, 0), ('R', 2, 1)),
        (('R', 3, 0), ('R', 4, 0), ('R', 4, 1)),
        (('R', 6, 0), ('R', 6, 1)),
    ),
    (
        (('A', 5, 3), ('A', 9, 2), ('A', 5, 2), ('A', 9, 6), ('A', 5, 0)),
        (),
        (('A', 9, 1), ('R', 0, 0), ('T', 0, 0)),
        (('A', 9, 7), ('R', 1, 0), ('A', 9, 5), ('A', 9, 4), ('A', 9, 0), ('A', 9, 3)),
        (),
        (),
        (('R', 3, 0), ('R', 3, 1)),
        (('R', 4, 1), ('R', 5, 0)),
        (('R', 6, 1),),
    ),
    (
        (('A', 2, 0), ('A', 10, 3), ('A', 6, 3), ('A', 6, 0), ('A', 6, 4), ('A', 10, 0), ('A', 6, 1)),
        (),
        (('A', 10, 6), ('R', 0, 0)),
        (),
        (('A', 10, 5), ('A', 10, 1), ('R', 1, 0), ('A', 10, 4), ('R', 2, 0), ('A', 10, 2), ('R', 2, 1), ('A', 10, 7), ('A', 10, 8)),
        (('R', 4, 1),),
        (),
        (),
        (('R', 6, 1), ('R', 5, 0), ('R', 7, 0), ('R', 7, 1)),
    ),
    (
        (('A', 7, 5), ('A', 11, 0), ('A', 7, 2), ('A', 3, 1), ('A', 3, 0)),
        (('A', 7, 1), ('A', 11, 2), ('A', 11, 5), ('A', 7, 0), ('A', 7, 4)),
        (),
        (('A', 11, 6),),
        (('A', 11, 7), ('R', 1, 0), ('R', 1, 1), ('A', 11, 4)),
        (('A', 11, 3), ('R', 3, 0), ('A', 11, 1), ('A', 11, 9), ('A', 11, 8)),
        (),
        (),
        (('R', 5, 1), ('R', 5, 0), ('R', 7, 0), ('R', 7, 1)),
    ),
)


def kernel(
    sizes, cols_hbm, targets_hbm, vals_hbm, out_ref,
    cols_ref, targets_ref, targets_up, right, pack, halo, lent, terms_out, terms_in,
    part, own, kept, recv,
    load_sem, pack_send, halo_recv, forward_send, lent_send, lent_recv, target_send, target_recv,
    term_send, term_recv, part_send, part_recv,
):
    rows, slots, outs, layers, groups, fine = sizes
    far = 2 * W
    layer = lax.axis_index("layer")
    col = lax.axis_index("col")
    group = lax.axis_index("row") * fine + col
    base = group * rows
    zero_at = rows * slots
    halo_at = zero_at + 1
    has_above = group < groups - 1
    has_below = group > 0

    def group_id(by):
        other = (group + by + groups) % groups
        return {"row": other // fine, "col": other % fine}

    below, above = group_id(-1), group_id(1)

    def sel(values):
        if len(set(values)) == 1:
            return jnp.int32(values[0])
        out = jnp.int32(values[-1])
        for n in range(len(values) - 1):
            out = jnp.where(layer == n, values[n], out)
        return out

    def among(which):
        which = sorted(set(which))
        if len(which) == layers:
            return None
        cond = layer == which[0]
        for n in which[1:]:
            cond = cond | (layer == n)
        return cond

    def guard(which, *more):
        conds = [c for c in (among(which), *more) if c is not None]
        def wrap(f):
            if not conds:
                f()
                return
            cond = conds[0]
            for c in conds[1:]:
                cond = cond & c
            pl.when(cond)(f)
        return wrap

    def find(row, column):
        slot = jnp.int32(0)
        hit = jnp.int32(0)
        for s in range(slots):
            same = (cols_ref[s, row] == column).astype(jnp.int32)
            slot = slot + s * same
            hit = hit + same
        return jnp.minimum(slot, slots - 1), hit

    def block_of(row, column):
        slot, hit = find(row, base + column)
        block = right[row * slots + slot]
        return jnp.where(hit > 0, block, jnp.zeros_like(block))

    lists, crossing = BELOW, LOCAL
    forwarded = {(rows + b, a) for a, b in FORWARD}
    down_most = max(len(x) for x in lists)
    cross_most = max(len(x) for x in crossing)
    lent_at = down_most + cross_most

    def at_of(k, t):
        return k // layers * far + t

    def down_copy(n):
        at = sel([at_of(*x[n]) if n < len(x) else 0 for x in lists])
        return pltpu.make_async_remote_copy(
            src_ref=pack.at[n], dst_ref=halo.at[at], send_sem=pack_send.at[n], recv_sem=halo_recv.at[at],
            device_id=below, device_id_type=MESH,
        )

    def down_has(n):
        return [m for m in range(layers) if n < len(lists[m])]

    def cross_copy(n):
        at = sel([at_of(*x[n]) if n < len(x) else 0 for x in crossing])
        to = sel([x[n][0] % layers if n < len(x) else 0 for x in crossing])
        return pltpu.make_async_remote_copy(
            src_ref=pack.at[down_most + n], dst_ref=halo.at[at],
            send_sem=pack_send.at[down_most + n], recv_sem=halo_recv.at[at],
            device_id={"layer": to}, device_id_type=MESH,
        )

    def cross_has(n):
        return [m for m in range(layers) if n < len(crossing[m])]

    def lent_copy(i):
        return pltpu.make_async_remote_copy(
            src_ref=pack.at[lent_at + i], dst_ref=lent.at[i], send_sem=lent_send.at[i], recv_sem=lent_recv.at[i],
            device_id=above, device_id_type=MESH,
        )

    def target_copy():
        return pltpu.make_async_remote_copy(
            src_ref=targets_ref, dst_ref=targets_up, send_sem=target_send, recv_sem=target_recv,
            device_id=above, device_id_type=MESH,
        )

    def forward_copy(n):
        a, b = FORWARD[n]
        return pltpu.make_async_remote_copy(
            src_ref=halo.at[at_of(rows + a, b)], dst_ref=halo.at[at_of(rows + b, a)],
            send_sem=forward_send.at[n], recv_sem=halo_recv.at[at_of(rows + b, a)],
            device_id={"layer": jnp.int32(b)}, device_id_type=MESH,
        )

    passed = [(k, t) for k in range(layers) for t in range(k - rows + W + 1)]

    def pass_copy(n):
        k, t = passed[n]
        return pltpu.make_async_remote_copy(
            src_ref=halo.at[at_of(k, t)], dst_ref=halo.at[at_of(rows + k, rows + t)],
            send_sem=forward_send.at[len(FORWARD) + n], recv_sem=halo_recv.at[at_of(rows + k, rows + t)],
            device_id=below, device_id_type=MESH,
        )

    def term_copy(n):
        return pltpu.make_async_remote_copy(
            src_ref=terms_out.at[n], dst_ref=terms_in.at[n], send_sem=term_send.at[n], recv_sem=term_recv.at[n],
            device_id=below, device_id_type=MESH,
        )

    def part_copy(at, recv_at, to):
        return pltpu.make_async_remote_copy(
            src_ref=part.at[at], dst_ref=recv.at[recv_at], send_sem=part_send.at[at], recv_sem=part_recv.at[recv_at],
            device_id={"layer": to}, device_id_type=MESH,
        )

    lx, ly = layer % 2, layer // 2
    flip_x, flip_y, both = ly * 2 + 1 - lx, (1 - ly) * 2 + lx, (1 - ly) * 2 + 1 - lx

    def first_copy(row):
        over_y = OVER_Y[row]
        to = sel([n ^ 2 if over_y[n] else n ^ 1 for n in range(layers)])
        return part_copy(row, sel([(3 if over_y[n] else 2) * rows + row for n in range(layers)]), to)

    def x_copy(row):
        return part_copy(rows + row, row, flip_x)

    def y_copy(row):
        return part_copy(2 * rows + row, rows + row, flip_y)

    def x_direct(row):
        return [n for n in range(layers) if not OVER_Y[row][n ^ 2]]

    def y_direct(row):
        return [n for n in range(layers) if OVER_Y[row][n ^ 1]]

    loads = [
        pltpu.make_async_copy(cols_hbm, cols_ref, load_sem.at[0]),
        pltpu.make_async_copy(targets_hbm, targets_ref, load_sem.at[1]),
        pltpu.make_async_copy(vals_hbm, right.at[pl.ds(0, rows * slots)], load_sem.at[2]),
    ]
    for load in loads:
        load.start()
    barrier = pltpu.get_barrier_semaphore()
    for r in range(1, layers):
        to = {"layer": (layer + r) % layers}
        pl.semaphore_signal(barrier, inc=1, device_id=to, device_id_type=MESH)

    @pl.when(has_below)
    def _():
        pl.semaphore_signal(barrier, inc=1, device_id=below, device_id_type=MESH)

    @pl.when(has_above)
    def _():
        pl.semaphore_signal(barrier, inc=1, device_id=above, device_id_type=MESH)

    right[zero_at] = jnp.zeros(right.shape[1:], right.dtype)
    for load in loads:
        load.wait()

    def cross_pack(n):
        @guard(cross_has(n), has_above)
        def _():
            row = sel([x[n][0] if n < len(x) else 0 for x in crossing])
            t = sel([x[n][1] if n < len(x) else 0 for x in crossing])
            pack[down_most + n] = block_of(row, rows + t).T

    def cross_start(n):
        @guard(cross_has(n), has_above)
        def _():
            cross_copy(n).start()

    def down_pack(n):
        @guard(down_has(n), has_below)
        def _():
            k = sel([x[n][0] if n < len(x) else 0 for x in lists])
            t = sel([x[n][1] if n < len(x) else 0 for x in lists])
            pack[n] = block_of(t, k - rows)

    def down_start(n):
        @guard(down_has(n), has_below)
        def _():
            down_copy(n).start()

    cross_pack(0)
    down_pack(0)
    pl.semaphore_wait(barrier, layers - 1 + has_below.astype(jnp.int32) + has_above.astype(jnp.int32))
    cross_start(0)
    down_start(0)

    def lend_start(cond):
        @pl.when(cond & has_above & (layer < 2))
        def _():
            target_copy().start()
            for i in range(2):
                @guard((0,) if i == 0 else (0, 1))
                def _(i=i):
                    pack[lent_at + i] = block_of(W + i, rows + layers + layer)
                    lent_copy(i).start()

    lend_start(col < fine - 1)

    for n in range(1, max(down_most, cross_most)):
        if n < cross_most:
            cross_pack(n)
            cross_start(n)
        if n < down_most:
            down_pack(n)
            down_start(n)

    right[halo_at + far + layer] = block_of(layers + layer, rows + layer).T

    def arrive(k, t):
        @pl.when(group < groups - 2 if t >= rows else has_above)
        def _():
            at = at_of(k, t)
            pltpu.make_async_remote_copy(
                src_ref=halo.at[at], dst_ref=halo.at[at], send_sem=pack_send.at[0], recv_sem=halo_recv.at[at],
                device_id=below, device_id_type=MESH,
            ).wait_recv()
            block = halo[at]
            right[halo_at + at] = block.T if (k, t) in forwarded else block
            for n, (a, b) in enumerate(FORWARD):
                if (rows + a, b) == (k, t):
                    forward_copy(n).start()
            if (k, t) in passed:
                @pl.when(has_below)
                def _():
                    pass_copy(passed.index((k, t))).start()

    def product(row, o):
        target = targets_ref[o, row]
        there = target - base
        near = jnp.clip(there, 0, rows - 1)
        t = there - rows
        total = None
        for s in range(slots):
            column = cols_ref[s, row]
            slot, hit = find(near, column)
            local_at = jnp.where(hit > 0, near * slots + slot, zero_at)
            place = column - base
            q = (place - layer) // layers
            reach = (place >= t + rows - W) & (place < rows + layers) & (t < far)
            far_at = jnp.where(reach, halo_at + q * far + t, zero_at)
            at = jnp.where(there < rows, local_at, far_at)
            at = jnp.where((target >= 0) & (column >= 0), at, zero_at)
            at = jnp.clip(at, 0, right.shape[0] - 1)
            term = lax.dot_general(
                right[row * slots + s], right[at], (((1,), (1,)), ((), ())),
                preferred_element_type=jnp.float32,
            )
            total = term if total is None else total + term
        if row >= W:
            lends = ((layer == 0) | ((layer == 1) & (row > W))) & has_above
            theirs = terms_in[(row - W) * outs + o].astype(jnp.float32)
            total = total + jnp.where(lends, theirs, jnp.zeros_like(theirs))
        slot, hit = find(row, target)
        mine = (hit > 0) & (target >= 0)
        block = right[row * slots + jnp.where(mine, slot, 0)].astype(jnp.float32)
        twice = jnp.where(mine, 2.0 * block, jnp.zeros_like(block))
        return twice - total

    def terms(i):
        def body(o, carry):
            target = targets_up[o, W + i]
            there = target - base
            near = jnp.clip(there, 0, rows - 1)
            slot, hit = find(near, base + layers + layer)
            local_at = jnp.where(hit > 0, near * slots + slot, zero_at)
            t = there - rows
            reach = layers + layer >= t + rows - W
            far_at = jnp.where(reach, halo_at + far + t, zero_at)
            at = jnp.where(there < rows, local_at, far_at)
            at = jnp.where((target >= 0) & (there >= 0), at, zero_at)
            at = jnp.clip(at, 0, right.shape[0] - 1)
            term = lax.dot_general(
                lent[i], right[at], (((1,), (1,)), ((), ())), preferred_element_type=jnp.float32,
            )
            terms_out[i * outs + o] = term.astype(terms_out.dtype)
            term_copy(i * outs + o).start()
            return carry
        lax.fori_loop(0, outs, body, 0)

    def settle(value, at, direct, copy):
        if not direct:
            kept[at - rows] = value
        elif len(direct) == layers:
            part[at] = value.astype(part.dtype)
            copy().start()
        else:
            kept[at - rows] = value

            @guard(direct)
            def _():
                part[at] = kept[at - rows].astype(part.dtype)
                copy().start()

    def one_row(row):
        part[row] = product(row, both).astype(part.dtype)
        first_copy(row).start()
        settle(product(row, flip_x), rows + row, x_direct(row), lambda: x_copy(row))
        settle(product(row, flip_y), 2 * rows + row, y_direct(row), lambda: y_copy(row))
        own[row] = product(row, layer)

    def relay(row, over_y):
        recv_at = (3 if over_y else 2) * rows + row
        at = (1 if over_y else 2) * rows + row
        part_copy(row, recv_at, flip_x).wait_recv()
        total = kept[at - rows] + recv[recv_at].astype(jnp.float32)
        part[at] = total.astype(part.dtype)
        (x_copy(row) if over_y else y_copy(row)).start()

    def lend(cond):
        @pl.when(cond & has_below)
        def _():
            target_copy().wait_recv()
            for i in range(2):
                @guard((0,) if i == 0 else (0, 1))
                def _(i=i):
                    lent_copy(i).wait_recv()
                    terms(i)

    for row in range(rows + 1):
        if row == FAR_LEND:
            lend_start(col == fine - 1)
        if row == FAR_TERMS:
            for n in range(2):
                @pl.when(layer == n)
                def _():
                    lend(col == 0)
        for n in range(layers):
            @pl.when(layer == n)
            def _(n=n):
                for what, first, second in STEPS[n][row]:
                    if what == "A":
                        arrive(first, second)
                    elif what == "R":
                        relay(first, second)
                    else:
                        lend(col > 0)
        if row == rows:
            break
        if row >= W:
            @guard((0,) if row == W else (0, 1), has_above)
            def _(row=row):
                for o in range(outs):
                    term_copy((row - W) * outs + o).wait_recv()
        one_row(row)

    for row in range(rows):
        part_copy(row, row, flip_x).wait_recv()
        part_copy(row, rows + row, flip_x).wait_recv()
        total = own[row] + recv[row].astype(jnp.float32)
        total = total + recv[rows + row].astype(jnp.float32)
        out_ref[row, 0] = total.astype(out_ref.dtype)

    for n in range(cross_most):
        guard(cross_has(n), has_above)(lambda n=n: cross_copy(n).wait_send())
    for n in range(down_most):
        guard(down_has(n), has_below)(lambda n=n: down_copy(n).wait_send())
    for n, (a, b) in enumerate(FORWARD):
        guard((a,), has_above)(lambda n=n: forward_copy(n).wait_send())
    for n, (k, t) in enumerate(passed):
        guard((k,), has_below, has_above)(lambda n=n: pass_copy(n).wait_send())

    @pl.when(has_above & (layer < 2))
    def _():
        target_copy().wait_send()
        for i in range(2):
            guard((0,) if i == 0 else (0, 1))(lambda i=i: lent_copy(i).wait_send())

    @pl.when(has_below & (layer < 2))
    def _():
        for i in range(2):
            @guard((0,) if i == 0 else (0, 1))
            def _(i=i):
                for o in range(outs):
                    term_copy(i * outs + o).wait_send()

    for row in range(rows):
        first_copy(row).wait_send()
        x_copy(row).wait_send()
        y_copy(row).wait_send()


def solution(mesh):
    layers = mesh.shape["layer"]
    fine = mesh.shape["col"]
    groups = mesh.shape["row"] * fine

    def per_device(cols, vals, outcols):
        rows, slots, size, _ = vals.shape
        outs = outcols.shape[1]
        assert rows == 2 * layers and rows == W + 2 and layers == 4 and outs == layers
        far = 2 * W
        block = (size, size)
        halo = 3 * far
        sent = 3 * rows
        packs = max(map(len, LOCAL)) + max(map(len, BELOW)) + 2
        return pl.pallas_call(
            functools.partial(kernel, (rows, slots, outs, layers, groups, fine)),
            out_shape=jax.ShapeDtypeStruct((rows, outs // layers) + block, jnp.bfloat16),
            in_specs=[
                pl.BlockSpec(memory_space=pl.ANY),
                pl.BlockSpec(memory_space=pl.ANY),
                pl.BlockSpec(memory_space=pl.ANY),
            ],
            out_specs=pl.BlockSpec(memory_space=pltpu.VMEM),
            scratch_shapes=[
                pltpu.SMEM(cols.shape[::-1], cols.dtype),
                pltpu.SMEM(outcols.shape[::-1], outcols.dtype),
                pltpu.SMEM(outcols.shape[::-1], outcols.dtype),
                pltpu.VMEM((rows * slots + 1 + halo,) + block, jnp.bfloat16),
                pltpu.VMEM((packs,) + block, jnp.bfloat16),
                pltpu.VMEM((halo,) + block, jnp.bfloat16),
                pltpu.VMEM((2,) + block, jnp.bfloat16),
                pltpu.VMEM((2 * outs,) + block, jnp.bfloat16),
                pltpu.VMEM((2 * outs,) + block, jnp.bfloat16),
                pltpu.VMEM((sent,) + block, jnp.bfloat16),
                pltpu.VMEM((rows,) + block, jnp.float32),
                pltpu.VMEM((2 * rows,) + block, jnp.float32),
                pltpu.VMEM((4 * rows,) + block, jnp.bfloat16),
                pltpu.SemaphoreType.DMA((3,)),
                pltpu.SemaphoreType.DMA((packs,)),
                pltpu.SemaphoreType.DMA((halo,)),
                pltpu.SemaphoreType.DMA((12,)),
                pltpu.SemaphoreType.DMA((2,)),
                pltpu.SemaphoreType.DMA((2,)),
                pltpu.SemaphoreType.DMA,
                pltpu.SemaphoreType.DMA,
                pltpu.SemaphoreType.DMA((2 * outs,)),
                pltpu.SemaphoreType.DMA((2 * outs,)),
                pltpu.SemaphoreType.DMA((sent,)),
                pltpu.SemaphoreType.DMA((4 * rows,)),
            ],
            compiler_params=pltpu.CompilerParams(collective_id=0, has_side_effects=True),
        )(cols.T, outcols.T, vals.reshape((rows * slots,) + block))

    in_specs = (
        P(("row", "col"), "layer"),
        P(("row", "col"), "layer", None, None),
        P(("row", "col"), None),
    )
    return jax.shard_map(
        per_device, mesh=mesh, in_specs=in_specs,
        out_specs=P(("row", "col"), "layer", None, None), check_vma=False,
    )
```

```python
import functools

import jax
import jax.numpy as jnp
from jax import lax
from jax.experimental import pallas as pl
from jax.experimental.pallas import tpu as pltpu
from jax.sharding import PartitionSpec as P

W = 6
MESH = pl.DeviceIdType.MESH

FAR_LEND, FAR_TERMS = 1, 4
UNITS = tuple((row, unit) for row in range(W) for unit in range(4)) + (
    (6, 0), (6, 1), (6, 2), (7, 0), (7, 1), (7, 2), (6, 3), (7, 3),
)
LOCAL = (
    ((5, 0), (6, 4), (2, 0), (7, 4)),
    ((7, 5), (3, 1), (4, 1), (7, 1), (6, 1)),
    ((4, 2), (5, 2), (7, 2)),
    ((6, 3), (5, 3)),
)
BELOW = (
    ((8, 4), (8, 1), (8, 0), (8, 2), (8, 6), (8, 5)),
    ((9, 2), (9, 7), (9, 1), (9, 5), (9, 4), (9, 3), (9, 6)),
    ((6, 0), (10, 3), (10, 5), (10, 1), (10, 6), (10, 2), (10, 7), (10, 4)),
    ((11, 0), (3, 0), (7, 0), (11, 4), (11, 7), (11, 5), (11, 3), (11, 6)),
)
FORWARD = ((1, 3), (0, 1), (3, 0), (2, 3), (0, 2))
OVER_Y = (
    (0, 0, 1, 0),
    (0, 1, 0, 1),
    (1, 0, 0, 0),
    (0, 0, 1, 1),
    (0, 0, 1, 1),
    (1, 1, 0, 0),
    (0, 1, 1, 1),
    (1, 0, 0, 0),
)
STEPS = (
    (
        (('A', 4, 2), ('A', 8, 4), ('A', 4, 1)),
        (),
        (),
        (),
        (),
        (),
        (('A', 8, 1),),
        (),
        (('T', 0, 0), ('A', 8, 0), ('A', 8, 3), ('R', 0, 0), ('A', 8, 2), ('R', 0, 1), ('A', 8, 6), ('A', 8, 5)),
        (),
        (),
        (('R', 2, 0),),
        (),
        (),
        (),
        (),
        (),
        (),
        (),
        (('R', 3, 1),),
        (),
        (),
        (),
        (),
        (),
        (('R', 3, 0),),
        (),
        (),
        (('R', 4, 0), ('R', 4, 1)),
        (),
        (('R', 6, 1),),
        (('R', 7, 0),),
        (),
    ),
    (
        (('A', 5, 0), ('A', 9, 2), ('A', 5, 3), ('A', 9, 7), ('A', 5, 2)),
        (),
        (),
        (),
        (),
        (),
        (('A', 9, 1), ('R', 0, 0)),
        (),
        (),
        (),
        (),
        (),
        (('A', 9, 5), ('R', 1, 0), ('T', 0, 0), ('A', 9, 4), ('R', 1, 1), ('A', 9, 0), ('A', 9, 3), ('A', 9, 6)),
        (),
        (),
        (),
        (('R', 3, 1),),
        (),
        (),
        (),
        (),
        (),
        (),
        (),
        (),
        (),
        (),
        (('R', 3, 0), ('R', 4, 1)),
        (),
        (('R', 4, 0),),
        (),
        (),
        (('R', 6, 0), ('R', 6, 1)),
    ),
    (
        (('A', 6, 3), ('A', 6, 0), ('A', 6, 4), ('A', 10, 3), ('A', 2, 0), ('A', 10, 5), ('A', 6, 1)),
        (),
        (),
        (),
        (),
        (('R', 0, 0),),
        (('A', 10, 1),),
        (),
        (),
        (),
        (),
        (),
        (('A', 10, 6),),
        (),
        (),
        (),
        (('A', 10, 2), ('A', 10, 0), ('R', 2, 0), ('A', 10, 7), ('R', 2, 1), ('A', 10, 4), ('A', 10, 8)),
        (),
        (),
        (),
        (),
        (),
        (),
        (),
        (),
        (),
        (),
        (),
        (),
        (),
        (),
        (),
        (('R', 5, 1), ('R', 5, 0), ('R', 7, 0), ('R', 7, 1)),
    ),
    (
        (('A', 7, 5), ('A', 11, 0), ('A', 3, 1), ('A', 3, 0), ('A', 7, 2)),
        (),
        (),
        (),
        (('A', 7, 1), ('A', 7, 0), ('A', 11, 2), ('A', 7, 4), ('A', 11, 4)),
        (),
        (),
        (),
        (),
        (),
        (('A', 11, 7),),
        (),
        (),
        (),
        (),
        (),
        (('A', 11, 5),),
        (),
        (),
        (),
        (('R', 1, 0), ('R', 1, 1), ('A', 11, 3), ('R', 2, 0), ('A', 11, 6), ('A', 11, 1), ('A', 11, 9), ('A', 11, 8)),
        (),
        (('R', 5, 1),),
        (),
        (),
        (),
        (),
        (),
        (),
        (),
        (),
        (),
        (('R', 5, 0), ('R', 6, 1), ('R', 7, 0)),
    ),
)


def kernel(
    sizes, cols_hbm, targets_hbm, vals_hbm, out_ref,
    cols_ref, targets_ref, targets_up, right, pack, halo, lent, terms_out, terms_in,
    part, own, kept, recv,
    load_sem, pack_send, halo_recv, forward_send, lent_send, lent_recv, target_send, target_recv,
    term_send, term_recv, part_send, part_recv,
):
    rows, slots, outs, layers, groups, fine = sizes
    far = 2 * W
    layer = lax.axis_index("layer")
    col = lax.axis_index("col")
    group = lax.axis_index("row") * fine + col
    base = group * rows
    zero_at = rows * slots
    halo_at = zero_at + 1
    has_above = group < groups - 1
    has_below = group > 0

    def group_id(by):
        other = (group + by + groups) % groups
        return {"row": other // fine, "col": other % fine}

    below, above = group_id(-1), group_id(1)

    def sel(values):
        if len(set(values)) == 1:
            return jnp.int32(values[0])
        out = jnp.int32(values[-1])
        for n in range(len(values) - 1):
            out = jnp.where(layer == n, values[n], out)
        return out

    def among(which):
        which = sorted(set(which))
        if len(which) == layers:
            return None
        cond = layer == which[0]
        for n in which[1:]:
            cond = cond | (layer == n)
        return cond

    def guard(which, *more):
        conds = [c for c in (among(which), *more) if c is not None]
        def wrap(f):
            if not conds:
                f()
                return
            cond = conds[0]
            for c in conds[1:]:
                cond = cond & c
            pl.when(cond)(f)
        return wrap

    def find(row, column):
        slot = jnp.int32(0)
        hit = jnp.int32(0)
        for s in range(slots):
            same = (cols_ref[s, row] == column).astype(jnp.int32)
            slot = slot + s * same
            hit = hit + same
        return jnp.minimum(slot, slots - 1), hit

    def block_of(row, column):
        slot, hit = find(row, base + column)
        block = right[row * slots + slot]
        return jnp.where(hit > 0, block, jnp.zeros_like(block))

    lists, crossing = BELOW, LOCAL
    forwarded = {(rows + b, a) for a, b in FORWARD}
    down_most = max(len(x) for x in lists)
    cross_most = max(len(x) for x in crossing)
    lent_at = down_most + cross_most

    def at_of(k, t):
        return k // layers * far + t

    def down_copy(n):
        at = sel([at_of(*x[n]) if n < len(x) else 0 for x in lists])
        return pltpu.make_async_remote_copy(
            src_ref=pack.at[n], dst_ref=halo.at[at], send_sem=pack_send.at[n], recv_sem=halo_recv.at[at],
            device_id=below, device_id_type=MESH,
        )

    def down_has(n):
        return [m for m in range(layers) if n < len(lists[m])]

    def cross_copy(n):
        at = sel([at_of(*x[n]) if n < len(x) else 0 for x in crossing])
        to = sel([x[n][0] % layers if n < len(x) else 0 for x in crossing])
        return pltpu.make_async_remote_copy(
            src_ref=pack.at[down_most + n], dst_ref=halo.at[at],
            send_sem=pack_send.at[down_most + n], recv_sem=halo_recv.at[at],
            device_id={"layer": to}, device_id_type=MESH,
        )

    def cross_has(n):
        return [m for m in range(layers) if n < len(crossing[m])]

    def lent_copy(i):
        return pltpu.make_async_remote_copy(
            src_ref=pack.at[lent_at + i], dst_ref=lent.at[i], send_sem=lent_send.at[i], recv_sem=lent_recv.at[i],
            device_id=above, device_id_type=MESH,
        )

    def target_copy():
        return pltpu.make_async_remote_copy(
            src_ref=targets_ref, dst_ref=targets_up, send_sem=target_send, recv_sem=target_recv,
            device_id=above, device_id_type=MESH,
        )

    def forward_copy(n):
        a, b = FORWARD[n]
        return pltpu.make_async_remote_copy(
            src_ref=halo.at[at_of(rows + a, b)], dst_ref=halo.at[at_of(rows + b, a)],
            send_sem=forward_send.at[n], recv_sem=halo_recv.at[at_of(rows + b, a)],
            device_id={"layer": jnp.int32(b)}, device_id_type=MESH,
        )

    passed = [(k, t) for k in range(layers) for t in range(k - rows + W + 1)]

    def pass_copy(n):
        k, t = passed[n]
        return pltpu.make_async_remote_copy(
            src_ref=halo.at[at_of(k, t)], dst_ref=halo.at[at_of(rows + k, rows + t)],
            send_sem=forward_send.at[len(FORWARD) + n], recv_sem=halo_recv.at[at_of(rows + k, rows + t)],
            device_id=below, device_id_type=MESH,
        )

    def term_copy(n):
        return pltpu.make_async_remote_copy(
            src_ref=terms_out.at[n], dst_ref=terms_in.at[n], send_sem=term_send.at[n], recv_sem=term_recv.at[n],
            device_id=below, device_id_type=MESH,
        )

    def part_copy(at, recv_at, to):
        return pltpu.make_async_remote_copy(
            src_ref=part.at[at], dst_ref=recv.at[recv_at], send_sem=part_send.at[at], recv_sem=part_recv.at[recv_at],
            device_id={"layer": to}, device_id_type=MESH,
        )

    lx, ly = layer % 2, layer // 2
    flip_x, flip_y, both = ly * 2 + 1 - lx, (1 - ly) * 2 + lx, (1 - ly) * 2 + 1 - lx

    def first_copy(row):
        over_y = OVER_Y[row]
        to = sel([n ^ 2 if over_y[n] else n ^ 1 for n in range(layers)])
        return part_copy(row, sel([(3 if over_y[n] else 2) * rows + row for n in range(layers)]), to)

    def x_copy(row):
        return part_copy(rows + row, row, flip_x)

    def y_copy(row):
        return part_copy(2 * rows + row, rows + row, flip_y)

    def x_direct(row):
        return [n for n in range(layers) if not OVER_Y[row][n ^ 2]]

    def y_direct(row):
        return [n for n in range(layers) if OVER_Y[row][n ^ 1]]

    loads = [
        pltpu.make_async_copy(cols_hbm, cols_ref, load_sem.at[0]),
        pltpu.make_async_copy(targets_hbm, targets_ref, load_sem.at[1]),
        pltpu.make_async_copy(vals_hbm, right.at[pl.ds(0, rows * slots)], load_sem.at[2]),
    ]
    for load in loads:
        load.start()
    barrier = pltpu.get_barrier_semaphore()
    for r in range(1, layers):
        to = {"layer": (layer + r) % layers}
        pl.semaphore_signal(barrier, inc=1, device_id=to, device_id_type=MESH)

    @pl.when(has_below)
    def _():
        pl.semaphore_signal(barrier, inc=1, device_id=below, device_id_type=MESH)

    @pl.when(has_above)
    def _():
        pl.semaphore_signal(barrier, inc=1, device_id=above, device_id_type=MESH)

    right[zero_at] = jnp.zeros(right.shape[1:], right.dtype)
    for load in loads:
        load.wait()

    def cross_pack(n):
        @guard(cross_has(n), has_above)
        def _():
            row = sel([x[n][0] if n < len(x) else 0 for x in crossing])
            t = sel([x[n][1] if n < len(x) else 0 for x in crossing])
            pack[down_most + n] = block_of(row, rows + t).T

    def cross_start(n):
        @guard(cross_has(n), has_above)
        def _():
            cross_copy(n).start()

    def down_pack(n):
        @guard(down_has(n), has_below)
        def _():
            k = sel([x[n][0] if n < len(x) else 0 for x in lists])
            t = sel([x[n][1] if n < len(x) else 0 for x in lists])
            pack[n] = block_of(t, k - rows)

    def down_start(n):
        @guard(down_has(n), has_below)
        def _():
            down_copy(n).start()

    cross_pack(0)
    down_pack(0)
    pl.semaphore_wait(barrier, layers - 1 + has_below.astype(jnp.int32) + has_above.astype(jnp.int32))
    cross_start(0)
    down_start(0)

    def lend_start(cond):
        @pl.when(cond & has_above & (layer < 2))
        def _():
            target_copy().start()
            for i in range(2):
                @guard((0,) if i == 0 else (0, 1))
                def _(i=i):
                    pack[lent_at + i] = block_of(W + i, rows + layers + layer)
                    lent_copy(i).start()

    lend_start(col < fine - 1)

    for n in range(1, max(down_most, cross_most)):
        if n < cross_most:
            cross_pack(n)
            cross_start(n)
        if n < down_most:
            down_pack(n)
            down_start(n)

    right[halo_at + far + layer] = block_of(layers + layer, rows + layer).T

    def arrive(k, t):
        @pl.when(group < groups - 2 if t >= rows else has_above)
        def _():
            at = at_of(k, t)
            pltpu.make_async_remote_copy(
                src_ref=halo.at[at], dst_ref=halo.at[at], send_sem=pack_send.at[0], recv_sem=halo_recv.at[at],
                device_id=below, device_id_type=MESH,
            ).wait_recv()
            block = halo[at]
            right[halo_at + at] = block.T if (k, t) in forwarded else block
            for n, (a, b) in enumerate(FORWARD):
                if (rows + a, b) == (k, t):
                    forward_copy(n).start()
            if (k, t) in passed:
                @pl.when(has_below)
                def _():
                    pass_copy(passed.index((k, t))).start()

    outputs = (both, flip_x, flip_y, layer)

    def product(row, unit):
        o = outputs[unit]
        target = targets_ref[o, row]
        there = target - base
        near = jnp.clip(there, 0, rows - 1)
        t = there - rows
        total = None
        for s in range(slots):
            column = cols_ref[s, row]
            slot, hit = find(near, column)
            local_at = jnp.where(hit > 0, near * slots + slot, zero_at)
            place = column - base
            q = (place - layer) // layers
            reach = (place >= t + rows - W) & (place < rows + layers) & (t < far)
            far_at = jnp.where(reach, halo_at + q * far + t, zero_at)
            at = jnp.where(there < rows, local_at, far_at)
            at = jnp.where((target >= 0) & (column >= 0), at, zero_at)
            at = jnp.clip(at, 0, right.shape[0] - 1)
            term = lax.dot_general(
                right[row * slots + s], right[at], (((1,), (1,)), ((), ())),
                preferred_element_type=jnp.float32,
            )
            total = term if total is None else total + term
        if row >= W:
            lends = ((layer == 0) | ((layer == 1) & (row > W))) & has_above
            theirs = terms_in[(row - W) * outs + unit].astype(jnp.float32)
            total = total + jnp.where(lends, theirs, jnp.zeros_like(theirs))
        slot, hit = find(row, target)
        mine = (hit > 0) & (target >= 0)
        block = right[row * slots + jnp.where(mine, slot, 0)].astype(jnp.float32)
        twice = jnp.where(mine, 2.0 * block, jnp.zeros_like(block))
        return twice - total

    def terms():
        for row, unit in UNITS:
            if row < W:
                continue

            @guard((0,) if row == W else (0, 1))
            def _(row=row, unit=unit):
                target = targets_up[outputs[unit], row]
                there = target - base
                near = jnp.clip(there, 0, rows - 1)
                slot, hit = find(near, base + layers + layer)
                local_at = jnp.where(hit > 0, near * slots + slot, zero_at)
                t = there - rows
                reach = layers + layer >= t + rows - W
                far_at = jnp.where(reach, halo_at + far + t, zero_at)
                at = jnp.where(there < rows, local_at, far_at)
                at = jnp.where((target >= 0) & (there >= 0), at, zero_at)
                at = jnp.clip(at, 0, right.shape[0] - 1)
                term = lax.dot_general(
                    lent[row - W], right[at], (((1,), (1,)), ((), ())), preferred_element_type=jnp.float32,
                )
                n = (row - W) * outs + unit
                terms_out[n] = term.astype(terms_out.dtype)
                term_copy(n).start()

    def settle(value, at, direct, copy):
        if not direct:
            kept[at - rows] = value
        elif len(direct) == layers:
            part[at] = value.astype(part.dtype)
            copy().start()
        else:
            kept[at - rows] = value

            @guard(direct)
            def _():
                part[at] = kept[at - rows].astype(part.dtype)
                copy().start()

    def one(row, unit):
        if row >= W:
            @guard((0,) if row == W else (0, 1), has_above)
            def _():
                term_copy((row - W) * outs + unit).wait_recv()
        value = product(row, unit)
        if unit == 0:
            part[row] = value.astype(part.dtype)
            first_copy(row).start()
        elif unit == 1:
            settle(value, rows + row, x_direct(row), lambda: x_copy(row))
        elif unit == 2:
            settle(value, 2 * rows + row, y_direct(row), lambda: y_copy(row))
        else:
            own[row] = value

    def relay(row, over_y):
        recv_at = (3 if over_y else 2) * rows + row
        at = (1 if over_y else 2) * rows + row
        part_copy(row, recv_at, flip_x).wait_recv()
        total = kept[at - rows] + recv[recv_at].astype(jnp.float32)
        part[at] = total.astype(part.dtype)
        (x_copy(row) if over_y else y_copy(row)).start()

    def lend(cond):
        @pl.when(cond & has_below)
        def _():
            target_copy().wait_recv()
            for i in range(2):
                guard((0,) if i == 0 else (0, 1))(lambda i=i: lent_copy(i).wait_recv())
            terms()

    for step in range(len(UNITS) + 1):
        row, unit = UNITS[step] if step < len(UNITS) else (rows, 0)
        if (row, unit) == (FAR_LEND, 0):
            lend_start(col == fine - 1)
        if (row, unit) == (FAR_TERMS, 0):
            for n in range(2):
                @pl.when(layer == n)
                def _():
                    lend(col == 0)
        for n in range(layers):
            if not STEPS[n][step]:
                continue

            @pl.when(layer == n)
            def _(n=n):
                for what, first, second in STEPS[n][step]:
                    if what == "A":
                        arrive(first, second)
                    elif what == "R":
                        relay(first, second)
                    else:
                        lend(col > 0)
        if step < len(UNITS):
            one(row, unit)

    for row in range(rows):
        part_copy(row, row, flip_x).wait_recv()
        part_copy(row, rows + row, flip_x).wait_recv()
        total = own[row] + recv[row].astype(jnp.float32)
        total = total + recv[rows + row].astype(jnp.float32)
        out_ref[row, 0] = total.astype(out_ref.dtype)

    for n in range(cross_most):
        guard(cross_has(n), has_above)(lambda n=n: cross_copy(n).wait_send())
    for n in range(down_most):
        guard(down_has(n), has_below)(lambda n=n: down_copy(n).wait_send())
    for n, (a, b) in enumerate(FORWARD):
        guard((a,), has_above)(lambda n=n: forward_copy(n).wait_send())
    for n, (k, t) in enumerate(passed):
        guard((k,), has_below, has_above)(lambda n=n: pass_copy(n).wait_send())

    @pl.when(has_above & (layer < 2))
    def _():
        target_copy().wait_send()
        for i in range(2):
            guard((0,) if i == 0 else (0, 1))(lambda i=i: lent_copy(i).wait_send())

    @pl.when(has_below & (layer < 2))
    def _():
        for i in range(2):
            @guard((0,) if i == 0 else (0, 1))
            def _(i=i):
                for o in range(outs):
                    term_copy(i * outs + o).wait_send()

    for row in range(rows):
        first_copy(row).wait_send()
        x_copy(row).wait_send()
        y_copy(row).wait_send()


def solution(mesh):
    layers = mesh.shape["layer"]
    fine = mesh.shape["col"]
    groups = mesh.shape["row"] * fine

    def per_device(cols, vals, outcols):
        rows, slots, size, _ = vals.shape
        outs = outcols.shape[1]
        assert rows == 2 * layers and rows == W + 2 and layers == 4 and outs == layers
        far = 2 * W
        block = (size, size)
        halo = 3 * far
        sent = 3 * rows
        packs = max(map(len, LOCAL)) + max(map(len, BELOW)) + 2
        return pl.pallas_call(
            functools.partial(kernel, (rows, slots, outs, layers, groups, fine)),
            out_shape=jax.ShapeDtypeStruct((rows, outs // layers) + block, jnp.bfloat16),
            in_specs=[
                pl.BlockSpec(memory_space=pl.ANY),
                pl.BlockSpec(memory_space=pl.ANY),
                pl.BlockSpec(memory_space=pl.ANY),
            ],
            out_specs=pl.BlockSpec(memory_space=pltpu.VMEM),
            scratch_shapes=[
                pltpu.SMEM(cols.shape[::-1], cols.dtype),
                pltpu.SMEM(outcols.shape[::-1], outcols.dtype),
                pltpu.SMEM(outcols.shape[::-1], outcols.dtype),
                pltpu.VMEM((rows * slots + 1 + halo,) + block, jnp.bfloat16),
                pltpu.VMEM((packs,) + block, jnp.bfloat16),
                pltpu.VMEM((halo,) + block, jnp.bfloat16),
                pltpu.VMEM((2,) + block, jnp.bfloat16),
                pltpu.VMEM((2 * outs,) + block, jnp.bfloat16),
                pltpu.VMEM((2 * outs,) + block, jnp.bfloat16),
                pltpu.VMEM((sent,) + block, jnp.bfloat16),
                pltpu.VMEM((rows,) + block, jnp.float32),
                pltpu.VMEM((2 * rows,) + block, jnp.float32),
                pltpu.VMEM((4 * rows,) + block, jnp.bfloat16),
                pltpu.SemaphoreType.DMA((3,)),
                pltpu.SemaphoreType.DMA((packs,)),
                pltpu.SemaphoreType.DMA((halo,)),
                pltpu.SemaphoreType.DMA((12,)),
                pltpu.SemaphoreType.DMA((2,)),
                pltpu.SemaphoreType.DMA((2,)),
                pltpu.SemaphoreType.DMA,
                pltpu.SemaphoreType.DMA,
                pltpu.SemaphoreType.DMA((2 * outs,)),
                pltpu.SemaphoreType.DMA((2 * outs,)),
                pltpu.SemaphoreType.DMA((sent,)),
                pltpu.SemaphoreType.DMA((4 * rows,)),
            ],
            compiler_params=pltpu.CompilerParams(
                collective_id=0, has_side_effects=True, vmem_limit_bytes=52 * 2 ** 20,
            ),
        )(
            pltpu.with_memory_space_constraint(cols.T, pltpu.HBM),
            pltpu.with_memory_space_constraint(outcols.T, pltpu.HBM),
            vals.reshape((rows * slots,) + block),
        )

    in_specs = (
        P(("row", "col"), "layer"),
        P(("row", "col"), "layer", None, None),
        P(("row", "col"), None),
    )
    return jax.shard_map(
        per_device, mesh=mesh, in_specs=in_specs,
        out_specs=P(("row", "col"), "layer", None, None), check_vma=False,
    )
```

```python
import functools

import jax
import jax.numpy as jnp
from jax import lax
from jax.experimental import pallas as pl
from jax.experimental.pallas import tpu as pltpu
from jax.sharding import PartitionSpec as P

W = 6
MESH = pl.DeviceIdType.MESH

FAR_LEND, FAR_TERMS = 1, 5
UNITS = tuple((row, unit) for row in range(W) for unit in range(4)) + (
    (6, 0), (6, 1), (6, 2), (7, 0), (7, 1), (7, 2), (6, 3), (7, 3),
)
LOCAL = (
    ((5, 0), (6, 4), (2, 0), (7, 4)),
    ((7, 5), (3, 1), (4, 1), (7, 1), (6, 1)),
    ((5, 2), (4, 2), (7, 2)),
    ((6, 3), (5, 3)),
)
BELOW = (
    ((8, 4), (8, 1), (8, 0), (8, 2), (8, 6), (8, 5)),
    ((9, 2), (9, 7), (9, 1), (9, 5), (9, 4), (9, 3), (9, 6)),
    ((6, 0), (10, 3), (10, 5), (10, 1), (10, 6), (10, 2), (10, 7), (10, 4)),
    ((11, 0), (3, 0), (7, 0), (11, 4), (11, 7), (11, 5), (11, 3), (11, 6)),
)
FORWARD = ((1, 3), (0, 1), (3, 0), (2, 3), (0, 2))
OVER_Y = (
    (0, 0, 1, 0),
    (0, 1, 0, 1),
    (1, 0, 0, 0),
    (0, 0, 1, 1),
    (0, 0, 1, 1),
    (1, 1, 0, 0),
    (0, 1, 1, 1),
    (1, 0, 0, 0),
)
STEPS = (
    (
        (('A', 8, 4), ('A', 4, 2), ('A', 4, 1)),
        (),
        (),
        (),
        (),
        (),
        (('A', 8, 1), ('A', 8, 0)),
        (),
        (('A', 8, 3), ('R', 0, 0), ('T', 0, 0), ('A', 8, 2), ('R', 0, 1), ('A', 8, 6), ('A', 8, 5)),
        (),
        (),
        (('R', 2, 0),),
        (),
        (),
        (),
        (),
        (),
        (),
        (),
        (('R', 3, 1),),
        (),
        (),
        (('R', 3, 0),),
        (),
        (),
        (),
        (),
        (),
        (('R', 4, 0), ('R', 4, 1)),
        (),
        (('R', 6, 1),),
        (('R', 7, 0),),
        (),
    ),
    (
        (('A', 5, 0), ('A', 9, 2), ('A', 5, 3), ('A', 9, 7), ('A', 5, 2)),
        (),
        (),
        (),
        (),
        (),
        (('A', 9, 1), ('R', 0, 0)),
        (),
        (),
        (),
        (),
        (),
        (('A', 9, 5), ('R', 1, 0), ('T', 0, 0), ('A', 9, 4), ('R', 1, 1), ('A', 9, 0), ('A', 9, 3), ('A', 9, 6)),
        (),
        (),
        (),
        (('R', 3, 1),),
        (),
        (),
        (),
        (),
        (),
        (),
        (),
        (),
        (),
        (),
        (('R', 3, 0), ('R', 4, 1)),
        (),
        (('R', 4, 0),),
        (),
        (),
        (('R', 6, 0), ('R', 6, 1)),
    ),
    (
        (('A', 6, 3), ('A', 6, 0), ('A', 6, 4), ('A', 10, 3), ('A', 2, 0), ('A', 10, 5), ('A', 6, 1)),
        (),
        (),
        (),
        (),
        (('R', 0, 0),),
        (('A', 10, 1),),
        (),
        (),
        (),
        (),
        (),
        (('A', 10, 6),),
        (),
        (),
        (),
        (('A', 10, 2), ('R', 2, 0), ('A', 10, 7), ('A', 10, 0), ('A', 10, 4), ('R', 2, 1), ('A', 10, 8)),
        (),
        (),
        (),
        (),
        (),
        (),
        (),
        (),
        (),
        (),
        (),
        (),
        (),
        (),
        (),
        (('R', 5, 1), ('R', 5, 0), ('R', 7, 0), ('R', 7, 1)),
    ),
    (
        (('A', 7, 5), ('A', 11, 0), ('A', 3, 1), ('A', 7, 2), ('A', 3, 0)),
        (),
        (),
        (),
        (('A', 7, 1), ('A', 7, 0), ('A', 11, 2), ('A', 7, 4), ('A', 11, 4)),
        (),
        (),
        (),
        (),
        (),
        (('A', 11, 7),),
        (),
        (),
        (),
        (),
        (),
        (('A', 11, 5),),
        (),
        (),
        (),
        (('R', 1, 0), ('R', 1, 1), ('A', 11, 3), ('R', 2, 0), ('A', 11, 6), ('A', 11, 1), ('A', 11, 9), ('A', 11, 8)),
        (),
        (('R', 5, 1),),
        (),
        (),
        (),
        (),
        (),
        (),
        (),
        (),
        (),
        (('R', 5, 0), ('R', 6, 1), ('R', 7, 0)),
    ),
)


def kernel(
    sizes, cols_hbm, targets_hbm, vals_hbm, out_ref,
    cols_ref, targets_ref, targets_up, right, pack, halo, lent, terms_out, terms_in,
    part, own, kept, recv,
    load_sem, pack_send, halo_recv, forward_send, lent_send, lent_recv, target_send, target_recv,
    term_send, term_recv, part_send, part_recv,
):
    rows, slots, outs, layers, groups, fine = sizes
    far = 2 * W
    layer = lax.axis_index("layer")
    col = lax.axis_index("col")
    group = lax.axis_index("row") * fine + col
    base = group * rows
    zero_at = rows * slots
    halo_at = zero_at + 1
    has_above = group < groups - 1
    has_below = group > 0

    def group_id(by):
        other = (group + by + groups) % groups
        return {"row": other // fine, "col": other % fine}

    below, above = group_id(-1), group_id(1)

    def sel(values):
        if len(set(values)) == 1:
            return jnp.int32(values[0])
        out = jnp.int32(values[-1])
        for n in range(len(values) - 1):
            out = jnp.where(layer == n, values[n], out)
        return out

    def among(which):
        which = sorted(set(which))
        if len(which) == layers:
            return None
        cond = layer == which[0]
        for n in which[1:]:
            cond = cond | (layer == n)
        return cond

    def guard(which, *more):
        conds = [c for c in (among(which), *more) if c is not None]
        def wrap(f):
            if not conds:
                f()
                return
            cond = conds[0]
            for c in conds[1:]:
                cond = cond & c
            pl.when(cond)(f)
        return wrap

    def find(row, column):
        slot = jnp.int32(0)
        hit = jnp.int32(0)
        for s in range(slots):
            same = (cols_ref[s, row] == column).astype(jnp.int32)
            slot = slot + s * same
            hit = hit + same
        return jnp.minimum(slot, slots - 1), hit

    def block_of(row, column):
        slot, hit = find(row, base + column)
        block = right[row * slots + slot]
        return jnp.where(hit > 0, block, jnp.zeros_like(block))

    lists, crossing = BELOW, LOCAL
    forwarded = {(rows + b, a) for a, b in FORWARD}
    down_most = max(len(x) for x in lists)
    cross_most = max(len(x) for x in crossing)
    lent_at = down_most + cross_most

    def at_of(k, t):
        return k // layers * far + t

    def down_copy(n):
        at = sel([at_of(*x[n]) if n < len(x) else 0 for x in lists])
        return pltpu.make_async_remote_copy(
            src_ref=pack.at[n], dst_ref=halo.at[at], send_sem=pack_send.at[n], recv_sem=halo_recv.at[at],
            device_id=below, device_id_type=MESH,
        )

    def down_has(n):
        return [m for m in range(layers) if n < len(lists[m])]

    def cross_copy(n):
        at = sel([at_of(*x[n]) if n < len(x) else 0 for x in crossing])
        to = sel([x[n][0] % layers if n < len(x) else 0 for x in crossing])
        return pltpu.make_async_remote_copy(
            src_ref=pack.at[down_most + n], dst_ref=halo.at[at],
            send_sem=pack_send.at[down_most + n], recv_sem=halo_recv.at[at],
            device_id={"layer": to}, device_id_type=MESH,
        )

    def cross_has(n):
        return [m for m in range(layers) if n < len(crossing[m])]

    def lent_copy(i):
        return pltpu.make_async_remote_copy(
            src_ref=pack.at[lent_at + i], dst_ref=lent.at[i], send_sem=lent_send.at[i], recv_sem=lent_recv.at[i],
            device_id=above, device_id_type=MESH,
        )

    def target_copy():
        return pltpu.make_async_remote_copy(
            src_ref=targets_ref, dst_ref=targets_up, send_sem=target_send, recv_sem=target_recv,
            device_id=above, device_id_type=MESH,
        )

    def forward_copy(n):
        a, b = FORWARD[n]
        return pltpu.make_async_remote_copy(
            src_ref=halo.at[at_of(rows + a, b)], dst_ref=halo.at[at_of(rows + b, a)],
            send_sem=forward_send.at[n], recv_sem=halo_recv.at[at_of(rows + b, a)],
            device_id={"layer": jnp.int32(b)}, device_id_type=MESH,
        )

    passed = [(k, t) for k in range(layers) for t in range(k - rows + W + 1)]

    def pass_copy(n):
        k, t = passed[n]
        return pltpu.make_async_remote_copy(
            src_ref=halo.at[at_of(k, t)], dst_ref=halo.at[at_of(rows + k, rows + t)],
            send_sem=forward_send.at[len(FORWARD) + n], recv_sem=halo_recv.at[at_of(rows + k, rows + t)],
            device_id=below, device_id_type=MESH,
        )

    def term_copy(n):
        return pltpu.make_async_remote_copy(
            src_ref=terms_out.at[n], dst_ref=terms_in.at[n], send_sem=term_send.at[n], recv_sem=term_recv.at[n],
            device_id=below, device_id_type=MESH,
        )

    def part_copy(at, recv_at, to):
        return pltpu.make_async_remote_copy(
            src_ref=part.at[at], dst_ref=recv.at[recv_at], send_sem=part_send.at[at], recv_sem=part_recv.at[recv_at],
            device_id={"layer": to}, device_id_type=MESH,
        )

    lx, ly = layer % 2, layer // 2
    flip_x, flip_y, both = ly * 2 + 1 - lx, (1 - ly) * 2 + lx, (1 - ly) * 2 + 1 - lx

    def first_copy(row):
        over_y = OVER_Y[row]
        to = sel([n ^ 2 if over_y[n] else n ^ 1 for n in range(layers)])
        return part_copy(row, sel([(3 if over_y[n] else 2) * rows + row for n in range(layers)]), to)

    def x_copy(row):
        return part_copy(rows + row, row, flip_x)

    def y_copy(row):
        return part_copy(2 * rows + row, rows + row, flip_y)

    def x_direct(row):
        return [n for n in range(layers) if not OVER_Y[row][n ^ 2]]

    def y_direct(row):
        return [n for n in range(layers) if OVER_Y[row][n ^ 1]]

    loads = [
        pltpu.make_async_copy(cols_hbm, cols_ref, load_sem.at[0]),
        pltpu.make_async_copy(targets_hbm, targets_ref, load_sem.at[1]),
        pltpu.make_async_copy(vals_hbm, right.at[pl.ds(0, rows * slots)], load_sem.at[2]),
    ]
    for load in loads:
        load.start()
    barrier = pltpu.get_barrier_semaphore()
    for r in range(1, layers):
        to = {"layer": (layer + r) % layers}
        pl.semaphore_signal(barrier, inc=1, device_id=to, device_id_type=MESH)

    @pl.when(has_below)
    def _():
        pl.semaphore_signal(barrier, inc=1, device_id=below, device_id_type=MESH)

    @pl.when(has_above)
    def _():
        pl.semaphore_signal(barrier, inc=1, device_id=above, device_id_type=MESH)

    right[zero_at] = jnp.zeros(right.shape[1:], right.dtype)
    for load in loads:
        load.wait()

    def cross_pack(n):
        @guard(cross_has(n), has_above)
        def _():
            row = sel([x[n][0] if n < len(x) else 0 for x in crossing])
            t = sel([x[n][1] if n < len(x) else 0 for x in crossing])
            pack[down_most + n] = block_of(row, rows + t).T

    def cross_start(n):
        @guard(cross_has(n), has_above)
        def _():
            cross_copy(n).start()

    def down_pack(n):
        @guard(down_has(n), has_below)
        def _():
            k = sel([x[n][0] if n < len(x) else 0 for x in lists])
            t = sel([x[n][1] if n < len(x) else 0 for x in lists])
            pack[n] = block_of(t, k - rows)

    def down_start(n):
        @guard(down_has(n), has_below)
        def _():
            down_copy(n).start()

    cross_pack(0)
    down_pack(0)
    pl.semaphore_wait(barrier, layers - 1 + has_below.astype(jnp.int32) + has_above.astype(jnp.int32))
    cross_start(0)
    down_start(0)

    def lend_start(cond):
        @pl.when(cond & has_above & (layer < 2))
        def _():
            target_copy().start()
            for i in range(2):
                @guard((0,) if i == 0 else (0, 1))
                def _(i=i):
                    pack[lent_at + i] = block_of(W + i, rows + layers + layer)
                    lent_copy(i).start()

    lend_start(col < fine - 1)

    for n in range(1, max(down_most, cross_most)):
        if n < cross_most:
            cross_pack(n)
            cross_start(n)
        if n < down_most:
            down_pack(n)
            down_start(n)

    right[halo_at + far + layer] = block_of(layers + layer, rows + layer).T

    def arrive(k, t):
        @pl.when(group < groups - 2 if t >= rows else has_above)
        def _():
            at = at_of(k, t)
            pltpu.make_async_remote_copy(
                src_ref=halo.at[at], dst_ref=halo.at[at], send_sem=pack_send.at[0], recv_sem=halo_recv.at[at],
                device_id=below, device_id_type=MESH,
            ).wait_recv()
            block = halo[at]
            right[halo_at + at] = block.T if (k, t) in forwarded else block
            for n, (a, b) in enumerate(FORWARD):
                if (rows + a, b) == (k, t):
                    forward_copy(n).start()
            if (k, t) in passed:
                @pl.when(has_below)
                def _():
                    pass_copy(passed.index((k, t))).start()

    outputs = (both, flip_x, flip_y, layer)

    def product(row, unit):
        o = outputs[unit]
        target = targets_ref[o, row]
        there = target - base
        near = jnp.clip(there, 0, rows - 1)
        t = there - rows
        total = None
        for s in range(slots):
            column = cols_ref[s, row]
            slot, hit = find(near, column)
            local_at = jnp.where(hit > 0, near * slots + slot, zero_at)
            place = column - base
            q = (place - layer) // layers
            reach = (place >= t + rows - W) & (place < rows + layers) & (t < far)
            far_at = jnp.where(reach, halo_at + q * far + t, zero_at)
            at = jnp.where(there < rows, local_at, far_at)
            at = jnp.where((target >= 0) & (column >= 0), at, zero_at)
            at = jnp.clip(at, 0, right.shape[0] - 1)
            term = lax.dot_general(
                right[row * slots + s], right[at], (((1,), (1,)), ((), ())),
                preferred_element_type=jnp.float32,
            )
            total = term if total is None else total + term
        if row >= W:
            lends = ((layer == 0) | ((layer == 1) & (row > W))) & has_above
            theirs = terms_in[(row - W) * outs + unit].astype(jnp.float32)
            total = total + jnp.where(lends, theirs, jnp.zeros_like(theirs))
        slot, hit = find(row, target)
        mine = (hit > 0) & (target >= 0)
        block = right[row * slots + jnp.where(mine, slot, 0)].astype(jnp.float32)
        twice = jnp.where(mine, 2.0 * block, jnp.zeros_like(block))
        return twice - total

    def terms():
        for row, unit in UNITS:
            if row < W:
                continue

            @guard((0,) if row == W else (0, 1))
            def _(row=row, unit=unit):
                target = targets_up[outputs[unit], row]
                there = target - base
                near = jnp.clip(there, 0, rows - 1)
                slot, hit = find(near, base + layers + layer)
                local_at = jnp.where(hit > 0, near * slots + slot, zero_at)
                t = there - rows
                reach = layers + layer >= t + rows - W
                far_at = jnp.where(reach, halo_at + far + t, zero_at)
                at = jnp.where(there < rows, local_at, far_at)
                at = jnp.where((target >= 0) & (there >= 0), at, zero_at)
                at = jnp.clip(at, 0, right.shape[0] - 1)
                term = lax.dot_general(
                    lent[row - W], right[at], (((1,), (1,)), ((), ())), preferred_element_type=jnp.float32,
                )
                n = (row - W) * outs + unit
                terms_out[n] = term.astype(terms_out.dtype)
                term_copy(n).start()

    def settle(value, at, direct, copy):
        if not direct:
            kept[at - rows] = value
        elif len(direct) == layers:
            part[at] = value.astype(part.dtype)
            copy().start()
        else:
            kept[at - rows] = value

            @guard(direct)
            def _():
                part[at] = kept[at - rows].astype(part.dtype)
                copy().start()

    def one(row, unit):
        if row >= W:
            @guard((0,) if row == W else (0, 1), has_above)
            def _():
                term_copy((row - W) * outs + unit).wait_recv()
        value = product(row, unit)
        if unit == 0:
            part[row] = value.astype(part.dtype)
            first_copy(row).start()
        elif unit == 1:
            settle(value, rows + row, x_direct(row), lambda: x_copy(row))
        elif unit == 2:
            settle(value, 2 * rows + row, y_direct(row), lambda: y_copy(row))
        else:
            own[row] = value

    def relay(row, over_y):
        recv_at = (3 if over_y else 2) * rows + row
        at = (1 if over_y else 2) * rows + row
        part_copy(row, recv_at, flip_x).wait_recv()
        total = kept[at - rows] + recv[recv_at].astype(jnp.float32)
        part[at] = total.astype(part.dtype)
        (x_copy(row) if over_y else y_copy(row)).start()

    def lend(cond):
        @pl.when(cond & has_below)
        def _():
            target_copy().wait_recv()
            for i in range(2):
                guard((0,) if i == 0 else (0, 1))(lambda i=i: lent_copy(i).wait_recv())
            terms()

    for step in range(len(UNITS) + 1):
        row, unit = UNITS[step] if step < len(UNITS) else (rows, 0)
        if (row, unit) == (FAR_LEND, 0):
            lend_start(col == fine - 1)
        if (row, unit) == (FAR_TERMS, 0):
            for n in range(2):
                @pl.when(layer == n)
                def _():
                    lend(col == 0)
        for n in range(layers):
            if not STEPS[n][step]:
                continue

            @pl.when(layer == n)
            def _(n=n):
                for what, first, second in STEPS[n][step]:
                    if what == "A":
                        arrive(first, second)
                    elif what == "R":
                        relay(first, second)
                    else:
                        lend(col > 0)
        if step < len(UNITS):
            one(row, unit)

    for row in range(rows):
        part_copy(row, row, flip_x).wait_recv()
        part_copy(row, rows + row, flip_x).wait_recv()
        total = own[row] + recv[row].astype(jnp.float32)
        total = total + recv[rows + row].astype(jnp.float32)
        out_ref[row, 0] = total.astype(out_ref.dtype)

    for n in range(cross_most):
        guard(cross_has(n), has_above)(lambda n=n: cross_copy(n).wait_send())
    for n in range(down_most):
        guard(down_has(n), has_below)(lambda n=n: down_copy(n).wait_send())
    for n, (a, b) in enumerate(FORWARD):
        guard((a,), has_above)(lambda n=n: forward_copy(n).wait_send())
    for n, (k, t) in enumerate(passed):
        guard((k,), has_below, has_above)(lambda n=n: pass_copy(n).wait_send())

    @pl.when(has_above & (layer < 2))
    def _():
        target_copy().wait_send()
        for i in range(2):
            guard((0,) if i == 0 else (0, 1))(lambda i=i: lent_copy(i).wait_send())

    @pl.when(has_below & (layer < 2))
    def _():
        for i in range(2):
            @guard((0,) if i == 0 else (0, 1))
            def _(i=i):
                for o in range(outs):
                    term_copy(i * outs + o).wait_send()

    for row in range(rows):
        first_copy(row).wait_send()
        x_copy(row).wait_send()
        y_copy(row).wait_send()


def solution(mesh):
    layers = mesh.shape["layer"]
    fine = mesh.shape["col"]
    groups = mesh.shape["row"] * fine

    def per_device(cols, vals, outcols):
        rows, slots, size, _ = vals.shape
        outs = outcols.shape[1]
        assert rows == 2 * layers and rows == W + 2 and layers == 4 and outs == layers
        far = 2 * W
        block = (size, size)
        halo = 3 * far
        sent = 3 * rows
        packs = max(map(len, LOCAL)) + max(map(len, BELOW)) + 2
        return pl.pallas_call(
            functools.partial(kernel, (rows, slots, outs, layers, groups, fine)),
            out_shape=jax.ShapeDtypeStruct((rows, outs // layers) + block, jnp.bfloat16),
            in_specs=[
                pl.BlockSpec(memory_space=pl.ANY),
                pl.BlockSpec(memory_space=pl.ANY),
                pl.BlockSpec(memory_space=pl.ANY),
            ],
            out_specs=pl.BlockSpec(memory_space=pltpu.VMEM),
            scratch_shapes=[
                pltpu.SMEM(cols.shape[::-1], cols.dtype),
                pltpu.SMEM(outcols.shape[::-1], outcols.dtype),
                pltpu.SMEM(outcols.shape[::-1], outcols.dtype),
                pltpu.VMEM((rows * slots + 1 + halo,) + block, jnp.bfloat16),
                pltpu.VMEM((packs,) + block, jnp.bfloat16),
                pltpu.VMEM((halo,) + block, jnp.bfloat16),
                pltpu.VMEM((2,) + block, jnp.bfloat16),
                pltpu.VMEM((2 * outs,) + block, jnp.bfloat16),
                pltpu.VMEM((2 * outs,) + block, jnp.bfloat16),
                pltpu.VMEM((sent,) + block, jnp.bfloat16),
                pltpu.VMEM((rows,) + block, jnp.float32),
                pltpu.VMEM((2 * rows,) + block, jnp.float32),
                pltpu.VMEM((4 * rows,) + block, jnp.bfloat16),
                pltpu.SemaphoreType.DMA((3,)),
                pltpu.SemaphoreType.DMA((packs,)),
                pltpu.SemaphoreType.DMA((halo,)),
                pltpu.SemaphoreType.DMA((12,)),
                pltpu.SemaphoreType.DMA((2,)),
                pltpu.SemaphoreType.DMA((2,)),
                pltpu.SemaphoreType.DMA,
                pltpu.SemaphoreType.DMA,
                pltpu.SemaphoreType.DMA((2 * outs,)),
                pltpu.SemaphoreType.DMA((2 * outs,)),
                pltpu.SemaphoreType.DMA((sent,)),
                pltpu.SemaphoreType.DMA((4 * rows,)),
            ],
            compiler_params=pltpu.CompilerParams(
                collective_id=0, has_side_effects=True, vmem_limit_bytes=52 * 2 ** 20,
            ),
        )(
            pltpu.with_memory_space_constraint(cols.T, pltpu.HBM),
            pltpu.with_memory_space_constraint(outcols.T, pltpu.HBM),
            vals.reshape((rows * slots,) + block),
        )

    in_specs = (
        P(("row", "col"), "layer"),
        P(("row", "col"), "layer", None, None),
        P(("row", "col"), None),
    )
    return jax.shard_map(
        per_device, mesh=mesh, in_specs=in_specs,
        out_specs=P(("row", "col"), "layer", None, None), check_vma=False,
    )
```

```python
import functools

import jax
import jax.numpy as jnp
from jax import lax
from jax.experimental import pallas as pl
from jax.experimental.pallas import tpu as pltpu
from jax.sharding import PartitionSpec as P

W = 6
MESH = pl.DeviceIdType.MESH

FAR_LEND, FAR_TERMS = 1, 5
UNITS = tuple((row, unit) for row in range(W) for unit in range(4)) + (
    (6, 0), (6, 1), (6, 2), (7, 0), (7, 1), (7, 2), (6, 3), (7, 3),
)
LOCAL = (
    ((5, 0), (6, 4), (2, 0), (7, 4)),
    ((7, 5), (3, 1), (4, 1), (7, 1), (6, 1)),
    ((5, 2), (4, 2), (7, 2)),
    ((6, 3), (5, 3)),
)
BELOW = (
    ((8, 4), (8, 1), (8, 0), (8, 2), (8, 6), (8, 5)),
    ((9, 2), (9, 7), (9, 1), (9, 5), (9, 4), (9, 3), (9, 6)),
    ((6, 0), (10, 3), (10, 5), (10, 1), (10, 6), (10, 2), (10, 7), (10, 4)),
    ((11, 0), (3, 0), (7, 0), (11, 4), (11, 7), (11, 5), (11, 3), (11, 6)),
)
FORWARD = ((1, 3), (0, 1), (3, 0), (2, 3), (0, 2))
OVER_Y = (
    (0, 0, 1, 0),
    (0, 1, 0, 1),
    (1, 0, 0, 0),
    (0, 0, 1, 1),
    (0, 0, 1, 1),
    (1, 1, 0, 0),
    (0, 1, 1, 1),
    (1, 0, 0, 0),
)
STEPS = (
    (
        (('A', 8, 4), ('A', 4, 2), ('A', 4, 1)),
        (),
        (),
        (),
        (),
        (),
        (('A', 8, 1), ('A', 8, 0)),
        (),
        (('A', 8, 3), ('R', 0, 0), ('T', 0, 0), ('A', 8, 2), ('R', 0, 1), ('A', 8, 6), ('A', 8, 5)),
        (),
        (),
        (('R', 2, 0),),
        (),
        (),
        (),
        (),
        (),
        (),
        (),
        (('R', 3, 1),),
        (),
        (),
        (('R', 3, 0),),
        (),
        (),
        (),
        (),
        (),
        (('R', 4, 0), ('R', 4, 1)),
        (),
        (('R', 7, 0), ('R', 6, 1)),
        (),
        (),
    ),
    (
        (('A', 5, 0), ('A', 9, 2), ('A', 5, 3), ('A', 9, 7), ('A', 5, 2)),
        (),
        (),
        (),
        (),
        (),
        (('A', 9, 1), ('R', 0, 0)),
        (),
        (),
        (),
        (),
        (),
        (('A', 9, 5), ('R', 1, 0), ('T', 0, 0), ('A', 9, 4), ('R', 1, 1), ('A', 9, 0), ('A', 9, 3), ('A', 9, 6)),
        (),
        (),
        (),
        (('R', 3, 1),),
        (),
        (),
        (),
        (),
        (),
        (),
        (),
        (),
        (),
        (),
        (('R', 3, 0),),
        (),
        (('R', 4, 0),),
        (),
        (('R', 4, 1),),
        (('R', 6, 0), ('R', 6, 1)),
    ),
    (
        (('A', 6, 3), ('A', 6, 0), ('A', 6, 4), ('A', 10, 3), ('A', 2, 0), ('A', 10, 5), ('A', 6, 1)),
        (),
        (),
        (),
        (),
        (('R', 0, 0),),
        (('A', 10, 1),),
        (),
        (),
        (),
        (),
        (),
        (('A', 10, 6),),
        (),
        (),
        (),
        (('A', 10, 2), ('R', 2, 0), ('A', 10, 7), ('A', 10, 0), ('A', 10, 4), ('R', 2, 1), ('A', 10, 8)),
        (),
        (),
        (),
        (),
        (),
        (),
        (),
        (),
        (),
        (),
        (),
        (),
        (),
        (),
        (),
        (('R', 5, 1), ('R', 5, 0), ('R', 7, 0), ('R', 7, 1)),
    ),
    (
        (('A', 7, 5), ('A', 11, 0), ('A', 3, 1), ('A', 7, 2), ('A', 3, 0)),
        (),
        (),
        (),
        (('A', 7, 1), ('A', 7, 0), ('A', 11, 2), ('A', 7, 4), ('A', 11, 4)),
        (),
        (),
        (),
        (),
        (),
        (('A', 11, 7),),
        (),
        (('R', 1, 1),),
        (),
        (),
        (('R', 1, 0),),
        (('A', 11, 5),),
        (),
        (),
        (),
        (('A', 11, 3), ('R', 2, 0), ('A', 11, 6), ('A', 11, 1), ('A', 11, 9), ('A', 11, 8)),
        (),
        (('R', 5, 1),),
        (),
        (),
        (),
        (),
        (),
        (),
        (),
        (),
        (),
        (('R', 5, 0), ('R', 6, 1), ('R', 7, 0)),
    ),
)


def kernel(
    sizes, cols_hbm, targets_hbm, vals_hbm, out_ref,
    cols_ref, targets_ref, targets_up, right, pack, halo, lent, terms_out, terms_in,
    part, own, kept, recv,
    load_sem, pack_send, halo_recv, forward_send, lent_send, lent_recv, target_send, target_recv,
    term_send, term_recv, part_send, part_recv,
):
    rows, slots, outs, layers, groups, fine = sizes
    far = 2 * W
    layer = lax.axis_index("layer")
    col = lax.axis_index("col")
    group = lax.axis_index("row") * fine + col
    base = group * rows
    zero_at = rows * slots
    halo_at = zero_at + 1
    has_above = group < groups - 1
    has_below = group > 0

    def group_id(by):
        other = (group + by + groups) % groups
        return {"row": other // fine, "col": other % fine}

    below, above = group_id(-1), group_id(1)

    def sel(values):
        if len(set(values)) == 1:
            return jnp.int32(values[0])
        out = jnp.int32(values[-1])
        for n in range(len(values) - 1):
            out = jnp.where(layer == n, values[n], out)
        return out

    def among(which):
        which = sorted(set(which))
        if len(which) == layers:
            return None
        cond = layer == which[0]
        for n in which[1:]:
            cond = cond | (layer == n)
        return cond

    def guard(which, *more):
        conds = [c for c in (among(which), *more) if c is not None]
        def wrap(f):
            if not conds:
                f()
                return
            cond = conds[0]
            for c in conds[1:]:
                cond = cond & c
            pl.when(cond)(f)
        return wrap

    def find(row, column):
        slot = jnp.int32(0)
        hit = jnp.int32(0)
        for s in range(slots):
            same = (cols_ref[s, row] == column).astype(jnp.int32)
            slot = slot + s * same
            hit = hit + same
        return jnp.minimum(slot, slots - 1), hit

    def block_of(row, column):
        slot, hit = find(row, base + column)
        block = right[row * slots + slot]
        return jnp.where(hit > 0, block, jnp.zeros_like(block))

    lists, crossing = BELOW, LOCAL
    forwarded = {(rows + b, a) for a, b in FORWARD}
    down_most = max(len(x) for x in lists)
    cross_most = max(len(x) for x in crossing)
    lent_at = down_most + cross_most

    def at_of(k, t):
        return k // layers * far + t

    def down_copy(n):
        at = sel([at_of(*x[n]) if n < len(x) else 0 for x in lists])
        return pltpu.make_async_remote_copy(
            src_ref=pack.at[n], dst_ref=halo.at[at], send_sem=pack_send.at[n], recv_sem=halo_recv.at[at],
            device_id=below, device_id_type=MESH,
        )

    def down_has(n):
        return [m for m in range(layers) if n < len(lists[m])]

    def cross_copy(n):
        at = sel([at_of(*x[n]) if n < len(x) else 0 for x in crossing])
        to = sel([x[n][0] % layers if n < len(x) else 0 for x in crossing])
        return pltpu.make_async_remote_copy(
            src_ref=pack.at[down_most + n], dst_ref=halo.at[at],
            send_sem=pack_send.at[down_most + n], recv_sem=halo_recv.at[at],
            device_id={"layer": to}, device_id_type=MESH,
        )

    def cross_has(n):
        return [m for m in range(layers) if n < len(crossing[m])]

    def lent_copy(i):
        return pltpu.make_async_remote_copy(
            src_ref=pack.at[lent_at + i], dst_ref=lent.at[i], send_sem=lent_send.at[i], recv_sem=lent_recv.at[i],
            device_id=above, device_id_type=MESH,
        )

    def target_copy():
        return pltpu.make_async_remote_copy(
            src_ref=targets_ref, dst_ref=targets_up, send_sem=target_send, recv_sem=target_recv,
            device_id=above, device_id_type=MESH,
        )

    def forward_copy(n):
        a, b = FORWARD[n]
        return pltpu.make_async_remote_copy(
            src_ref=halo.at[at_of(rows + a, b)], dst_ref=halo.at[at_of(rows + b, a)],
            send_sem=forward_send.at[n], recv_sem=halo_recv.at[at_of(rows + b, a)],
            device_id={"layer": jnp.int32(b)}, device_id_type=MESH,
        )

    passed = [(k, t) for k in range(layers) for t in range(k - rows + W + 1)]

    def pass_copy(n):
        k, t = passed[n]
        return pltpu.make_async_remote_copy(
            src_ref=halo.at[at_of(k, t)], dst_ref=halo.at[at_of(rows + k, rows + t)],
            send_sem=forward_send.at[len(FORWARD) + n], recv_sem=halo_recv.at[at_of(rows + k, rows + t)],
            device_id=below, device_id_type=MESH,
        )

    def term_copy(n):
        return pltpu.make_async_remote_copy(
            src_ref=terms_out.at[n], dst_ref=terms_in.at[n], send_sem=term_send.at[n], recv_sem=term_recv.at[n],
            device_id=below, device_id_type=MESH,
        )

    def part_copy(at, recv_at, to):
        return pltpu.make_async_remote_copy(
            src_ref=part.at[at], dst_ref=recv.at[recv_at], send_sem=part_send.at[at], recv_sem=part_recv.at[recv_at],
            device_id={"layer": to}, device_id_type=MESH,
        )

    lx, ly = layer % 2, layer // 2
    flip_x, flip_y, both = ly * 2 + 1 - lx, (1 - ly) * 2 + lx, (1 - ly) * 2 + 1 - lx

    def first_copy(row):
        over_y = OVER_Y[row]
        to = sel([n ^ 2 if over_y[n] else n ^ 1 for n in range(layers)])
        return part_copy(row, sel([(3 if over_y[n] else 2) * rows + row for n in range(layers)]), to)

    def x_copy(row):
        return part_copy(rows + row, row, flip_x)

    def y_copy(row):
        return part_copy(2 * rows + row, rows + row, flip_y)

    def x_direct(row):
        return [n for n in range(layers) if not OVER_Y[row][n ^ 2]]

    def y_direct(row):
        return [n for n in range(layers) if OVER_Y[row][n ^ 1]]

    loads = [
        pltpu.make_async_copy(cols_hbm, cols_ref, load_sem.at[0]),
        pltpu.make_async_copy(targets_hbm, targets_ref, load_sem.at[1]),
        pltpu.make_async_copy(vals_hbm, right.at[pl.ds(0, rows * slots)], load_sem.at[2]),
    ]
    for load in loads:
        load.start()
    barrier = pltpu.get_barrier_semaphore()
    for r in range(1, layers):
        to = {"layer": (layer + r) % layers}
        pl.semaphore_signal(barrier, inc=1, device_id=to, device_id_type=MESH)

    @pl.when(has_below)
    def _():
        pl.semaphore_signal(barrier, inc=1, device_id=below, device_id_type=MESH)

    @pl.when(has_above)
    def _():
        pl.semaphore_signal(barrier, inc=1, device_id=above, device_id_type=MESH)

    right[zero_at] = jnp.zeros(right.shape[1:], right.dtype)
    for load in loads:
        load.wait()

    def cross_pack(n):
        @guard(cross_has(n), has_above)
        def _():
            row = sel([x[n][0] if n < len(x) else 0 for x in crossing])
            t = sel([x[n][1] if n < len(x) else 0 for x in crossing])
            pack[down_most + n] = block_of(row, rows + t).T

    def cross_start(n):
        @guard(cross_has(n), has_above)
        def _():
            cross_copy(n).start()

    def down_pack(n):
        @guard(down_has(n), has_below)
        def _():
            k = sel([x[n][0] if n < len(x) else 0 for x in lists])
            t = sel([x[n][1] if n < len(x) else 0 for x in lists])
            pack[n] = block_of(t, k - rows)

    def down_start(n):
        @guard(down_has(n), has_below)
        def _():
            down_copy(n).start()

    cross_pack(0)
    down_pack(0)
    pl.semaphore_wait(barrier, layers - 1 + has_below.astype(jnp.int32) + has_above.astype(jnp.int32))
    cross_start(0)
    down_start(0)

    def lend_start(cond):
        @pl.when(cond & has_above & (layer < 2))
        def _():
            target_copy().start()
            for i in range(2):
                @guard((0,) if i == 0 else (0, 1))
                def _(i=i):
                    pack[lent_at + i] = block_of(W + i, rows + layers + layer)
                    lent_copy(i).start()

    lend_start(col < fine - 1)

    for n in range(1, max(down_most, cross_most)):
        if n < cross_most:
            cross_pack(n)
            cross_start(n)
        if n < down_most:
            down_pack(n)
            down_start(n)

    right[halo_at + far + layer] = block_of(layers + layer, rows + layer).T

    def arrive(k, t):
        @pl.when(group < groups - 2 if t >= rows else has_above)
        def _():
            at = at_of(k, t)
            pltpu.make_async_remote_copy(
                src_ref=halo.at[at], dst_ref=halo.at[at], send_sem=pack_send.at[0], recv_sem=halo_recv.at[at],
                device_id=below, device_id_type=MESH,
            ).wait_recv()
            block = halo[at]
            right[halo_at + at] = block.T if (k, t) in forwarded else block
            for n, (a, b) in enumerate(FORWARD):
                if (rows + a, b) == (k, t):
                    forward_copy(n).start()
            if (k, t) in passed:
                @pl.when(has_below)
                def _():
                    pass_copy(passed.index((k, t))).start()

    outputs = (both, flip_x, flip_y, layer)

    def product(row, unit):
        o = outputs[unit]
        target = targets_ref[o, row]
        there = target - base
        near = jnp.clip(there, 0, rows - 1)
        t = there - rows
        total = None
        for s in range(slots):
            column = cols_ref[s, row]
            slot, hit = find(near, column)
            local_at = jnp.where(hit > 0, near * slots + slot, zero_at)
            place = column - base
            q = (place - layer) // layers
            reach = (place >= t + rows - W) & (place < rows + layers) & (t < far)
            far_at = jnp.where(reach, halo_at + q * far + t, zero_at)
            at = jnp.where(there < rows, local_at, far_at)
            at = jnp.where((target >= 0) & (column >= 0), at, zero_at)
            at = jnp.clip(at, 0, right.shape[0] - 1)
            term = lax.dot_general(
                right[row * slots + s], right[at], (((1,), (1,)), ((), ())),
                preferred_element_type=jnp.float32,
            )
            total = term if total is None else total + term
        if row >= W:
            lends = ((layer == 0) | ((layer == 1) & (row > W))) & has_above
            theirs = terms_in[(row - W) * outs + unit].astype(jnp.float32)
            total = total + jnp.where(lends, theirs, jnp.zeros_like(theirs))
        slot, hit = find(row, target)
        mine = (hit > 0) & (target >= 0)
        block = right[row * slots + jnp.where(mine, slot, 0)].astype(jnp.float32)
        twice = jnp.where(mine, 2.0 * block, jnp.zeros_like(block))
        return twice - total

    def terms():
        for row, unit in UNITS:
            if row < W:
                continue

            @guard((0,) if row == W else (0, 1))
            def _(row=row, unit=unit):
                target = targets_up[outputs[unit], row]
                there = target - base
                near = jnp.clip(there, 0, rows - 1)
                slot, hit = find(near, base + layers + layer)
                local_at = jnp.where(hit > 0, near * slots + slot, zero_at)
                t = there - rows
                reach = layers + layer >= t + rows - W
                far_at = jnp.where(reach, halo_at + far + t, zero_at)
                at = jnp.where(there < rows, local_at, far_at)
                at = jnp.where((target >= 0) & (there >= 0), at, zero_at)
                at = jnp.clip(at, 0, right.shape[0] - 1)
                term = lax.dot_general(
                    lent[row - W], right[at], (((1,), (1,)), ((), ())), preferred_element_type=jnp.float32,
                )
                n = (row - W) * outs + unit
                terms_out[n] = term.astype(terms_out.dtype)
                term_copy(n).start()

    def settle(value, at, direct, copy):
        if not direct:
            kept[at - rows] = value
        elif len(direct) == layers:
            part[at] = value.astype(part.dtype)
            copy().start()
        else:
            kept[at - rows] = value

            @guard(direct)
            def _():
                part[at] = kept[at - rows].astype(part.dtype)
                copy().start()

    def one(row, unit):
        if row >= W:
            @guard((0,) if row == W else (0, 1), has_above)
            def _():
                term_copy((row - W) * outs + unit).wait_recv()
        value = product(row, unit)
        if unit == 0:
            part[row] = value.astype(part.dtype)
            first_copy(row).start()
        elif unit == 1:
            settle(value, rows + row, x_direct(row), lambda: x_copy(row))
        elif unit == 2:
            settle(value, 2 * rows + row, y_direct(row), lambda: y_copy(row))
        else:
            own[row] = value

    def relay(row, over_y):
        recv_at = (3 if over_y else 2) * rows + row
        at = (1 if over_y else 2) * rows + row
        part_copy(row, recv_at, flip_x).wait_recv()
        total = kept[at - rows] + recv[recv_at].astype(jnp.float32)
        part[at] = total.astype(part.dtype)
        (x_copy(row) if over_y else y_copy(row)).start()

    def lend(cond):
        @pl.when(cond & has_below)
        def _():
            target_copy().wait_recv()
            for i in range(2):
                guard((0,) if i == 0 else (0, 1))(lambda i=i: lent_copy(i).wait_recv())
            terms()

    for step in range(len(UNITS) + 1):
        row, unit = UNITS[step] if step < len(UNITS) else (rows, 0)
        if (row, unit) == (FAR_LEND, 0):
            lend_start(col == fine - 1)
        if (row, unit) == (FAR_TERMS, 0):
            for n in range(2):
                @pl.when(layer == n)
                def _():
                    lend(col == 0)
        for n in range(layers):
            if not STEPS[n][step]:
                continue

            @pl.when(layer == n)
            def _(n=n):
                for what, first, second in STEPS[n][step]:
                    if what == "A":
                        arrive(first, second)
                    elif what == "R":
                        relay(first, second)
                    else:
                        lend(col > 0)
        if step < len(UNITS):
            one(row, unit)

    for row in range(rows):
        part_copy(row, row, flip_x).wait_recv()
        part_copy(row, rows + row, flip_x).wait_recv()
        total = own[row] + recv[row].astype(jnp.float32)
        total = total + recv[rows + row].astype(jnp.float32)
        out_ref[row, 0] = total.astype(out_ref.dtype)

    for n in range(cross_most):
        guard(cross_has(n), has_above)(lambda n=n: cross_copy(n).wait_send())
    for n in range(down_most):
        guard(down_has(n), has_below)(lambda n=n: down_copy(n).wait_send())
    for n, (a, b) in enumerate(FORWARD):
        guard((a,), has_above)(lambda n=n: forward_copy(n).wait_send())
    for n, (k, t) in enumerate(passed):
        guard((k,), has_below, has_above)(lambda n=n: pass_copy(n).wait_send())

    @pl.when(has_above & (layer < 2))
    def _():
        target_copy().wait_send()
        for i in range(2):
            guard((0,) if i == 0 else (0, 1))(lambda i=i: lent_copy(i).wait_send())

    @pl.when(has_below & (layer < 2))
    def _():
        for i in range(2):
            @guard((0,) if i == 0 else (0, 1))
            def _(i=i):
                for o in range(outs):
                    term_copy(i * outs + o).wait_send()

    for row in range(rows):
        first_copy(row).wait_send()
        x_copy(row).wait_send()
        y_copy(row).wait_send()


def solution(mesh):
    layers = mesh.shape["layer"]
    fine = mesh.shape["col"]
    groups = mesh.shape["row"] * fine

    def per_device(cols, vals, outcols):
        rows, slots, size, _ = vals.shape
        outs = outcols.shape[1]
        assert rows == 2 * layers and rows == W + 2 and layers == 4 and outs == layers
        far = 2 * W
        block = (size, size)
        halo = 3 * far
        sent = 3 * rows
        packs = max(map(len, LOCAL)) + max(map(len, BELOW)) + 2
        return pl.pallas_call(
            functools.partial(kernel, (rows, slots, outs, layers, groups, fine)),
            out_shape=jax.ShapeDtypeStruct((rows, outs // layers) + block, jnp.bfloat16),
            in_specs=[
                pl.BlockSpec(memory_space=pl.ANY),
                pl.BlockSpec(memory_space=pl.ANY),
                pl.BlockSpec(memory_space=pl.ANY),
            ],
            out_specs=pl.BlockSpec(memory_space=pltpu.VMEM),
            scratch_shapes=[
                pltpu.SMEM(cols.shape[::-1], cols.dtype),
                pltpu.SMEM(outcols.shape[::-1], outcols.dtype),
                pltpu.SMEM(outcols.shape[::-1], outcols.dtype),
                pltpu.VMEM((rows * slots + 1 + halo,) + block, jnp.bfloat16),
                pltpu.VMEM((packs,) + block, jnp.bfloat16),
                pltpu.VMEM((halo,) + block, jnp.bfloat16),
                pltpu.VMEM((2,) + block, jnp.bfloat16),
                pltpu.VMEM((2 * outs,) + block, jnp.bfloat16),
                pltpu.VMEM((2 * outs,) + block, jnp.bfloat16),
                pltpu.VMEM((sent,) + block, jnp.bfloat16),
                pltpu.VMEM((rows,) + block, jnp.float32),
                pltpu.VMEM((2 * rows,) + block, jnp.float32),
                pltpu.VMEM((4 * rows,) + block, jnp.bfloat16),
                pltpu.SemaphoreType.DMA((3,)),
                pltpu.SemaphoreType.DMA((packs,)),
                pltpu.SemaphoreType.DMA((halo,)),
                pltpu.SemaphoreType.DMA((12,)),
                pltpu.SemaphoreType.DMA((2,)),
                pltpu.SemaphoreType.DMA((2,)),
                pltpu.SemaphoreType.DMA,
                pltpu.SemaphoreType.DMA,
                pltpu.SemaphoreType.DMA((2 * outs,)),
                pltpu.SemaphoreType.DMA((2 * outs,)),
                pltpu.SemaphoreType.DMA((sent,)),
                pltpu.SemaphoreType.DMA((4 * rows,)),
            ],
            compiler_params=pltpu.CompilerParams(
                collective_id=0, has_side_effects=True, vmem_limit_bytes=52 * 2 ** 20,
            ),
        )(
            pltpu.with_memory_space_constraint(cols.T, pltpu.HBM),
            pltpu.with_memory_space_constraint(outcols.T, pltpu.HBM),
            vals.reshape((rows * slots,) + block),
        )

    in_specs = (
        P(("row", "col"), "layer"),
        P(("row", "col"), "layer", None, None),
        P(("row", "col"), None),
    )
    return jax.shard_map(
        per_device, mesh=mesh, in_specs=in_specs,
        out_specs=P(("row", "col"), "layer", None, None), check_vma=False,
    )
```
